512 devices in a mesh: tm: 512 (over x, z, y, core).
Axes of the slice: x: 4, y: 8, z: 8, core: 2. Of those that a mesh axis runs over, the one named last changes fastest.
Arguments:
- inv_diag: float32 [512, 384, 384], P('tm'), may hold values from -0.4 to 4.4, as said below
- low_coupling: float32 [512, 384, 384], P('tm'), may hold values from -0.09375 to 0.09375
- up_coupling: float32 [512, 384, 384], P('tm'), may hold values from -0.09375 to 0.09375
Outputs:
- diag_inverse: float32 [512, 384, 384], P('tm')
- cross_inverse: float32 [512, 384, 384], P('tm')
The draws below stay inside these ranges and needn't reach their ends.
Inputs may be any that keep to these rules, and one draw needn't show every extreme that they name: `inv_diag`: each block is symmetric.
All inputs are finite; a program needn't handle non-finite values.
Results may differ from the reference program's by a relative error of at most 0.00012.
Values sent between devices are 32-bit elements; how exact they have to be, the bound alone decides.
A program may use at most 64 MiB of HBM per device.

```python
import math
import jax
import jax.numpy as jnp
import numpy as np
from jax import lax

B = 384
CHAIN = 512
BLOCKS = 512


def draw_inv_diag(key, part):
    first, second = jax.random.split(key, 2)
    noise = jnp.clip(jax.random.normal(first, (BLOCKS, B, B), jnp.float32), -4.0, 4.0)
    symmetric = (noise + jnp.swapaxes(noise, 1, 2)) * (0.35 / math.sqrt(B))
    identity = jnp.eye(B, dtype=jnp.float32)
    diagonal = jax.random.uniform(second, (BLOCKS, B), jnp.float32, 1.5, 3.0)
    symmetric = jnp.clip(symmetric, -0.36, 0.36)
    return symmetric + diagonal[:, :, None] * identity


def shard_levels(key, shape, cuts, least, largest):
    def one(axis_at, blocks):
        draws = jax.random.uniform(jax.random.fold_in(jax.random.fold_in(key, 6), axis_at), (blocks,), jnp.float32, least / len(cuts), largest / len(cuts))
        return jnp.repeat(jnp.exp(draws), shape[axis_at] // blocks).reshape((-1,) + (1,) * (len(shape) - axis_at - 1))

    loudness = one(*cuts[0])
    for cut in cuts[1:]:
        loudness = loudness * one(*cut)
    return loudness


def normal_values(stream_key, extent, spread, reach, pieces=(), held_as=jnp.bfloat16):
    drawn = spread * jax.random.normal(stream_key, extent, jnp.float32)
    if pieces:
        drawn = drawn * shard_levels(stream_key, extent, pieces, -0.22, 0.18)
    return jnp.clip(drawn, -reach, reach).astype(held_as)


def setup_inputs(seed: int = 0) -> dict:
    arg_keys = jax.random.split(jax.random.key(seed), 4)
    return {
        "inv_diag": draw_inv_diag(jax.random.fold_in(arg_keys[3], 71), 0),
        "low_coupling": normal_values(arg_keys[1], (BLOCKS, B, B), (10 * B) ** -0.5, 0.09375, ((0, 512),), jnp.float32),
        "up_coupling": normal_values(arg_keys[2], (BLOCKS, B, B), (10 * B) ** -0.5, 0.09375, ((0, 512),), jnp.float32),
    }


row_offset = 3


def multiply(left, right):
    return jnp.einsum("cnij,cnjk->cnik", left, right, precision=lax.Precision.HIGHEST)


def multiply_trans(left, right):
    return jnp.einsum("cnij,cnkj->cnik", left, right, precision=lax.Precision.HIGHEST)


def reference(inv_diag, low_coupling, up_coupling):
    levels = CHAIN.bit_length() - 1
    inverses = jnp.roll(inv_diag, row_offset, axis=0).reshape(1, CHAIN, B, B)
    lowers = jnp.roll(low_coupling, row_offset, axis=0).reshape(1, CHAIN, B, B)
    uppers = jnp.roll(up_coupling, row_offset, axis=0).reshape(1, CHAIN, B, B)
    sigma = jnp.zeros((1, CHAIN + 1, B, B), jnp.float32)
    sigma = sigma.at[:, 0].set(inverses[:, 0])
    cross = jnp.zeros((1, CHAIN + 1, B, B), jnp.float32)
    newest = jnp.zeros((1, CHAIN + 1, B, B), jnp.float32)
    for step_num in range(levels):
        stride = CHAIN // (2 ** (step_num + 1))
        eliminated = np.arange(stride, CHAIN, 2 * stride)
        below_idx = eliminated - stride
        above_idx = np.minimum(eliminated + stride, CHAIN)
        inverse = inverses[:, eliminated]
        g_mat = multiply(inverse, lowers[:, eliminated])
        h_mat = multiply(inverse, uppers[:, eliminated])
        sigma_low = sigma[:, below_idx]
        sigma_high = sigma[:, above_idx]
        sigma_ba = newest[:, above_idx]
        sigma_ab = jnp.swapaxes(sigma_ba, 2, 3)
        part_low = -(multiply(g_mat, sigma_low) + multiply(h_mat, sigma_ba))
        part_high = -(multiply(g_mat, sigma_ab) + multiply(h_mat, sigma_high))
        sigma_tt = inverse - multiply_trans(g_mat, part_low) - multiply_trans(h_mat, part_high)
        sigma = sigma.at[:, eliminated].set(sigma_tt)
        cross = cross.at[:, eliminated].set(part_low)
        newest = newest.at[:, eliminated].set(part_low)
        inside = eliminated + stride < CHAIN
        targets = (eliminated + stride)[inside]
        newest = newest.at[:, targets].set(jnp.swapaxes(part_high[:, inside], 2, 3))
    diag_out = jnp.roll(sigma[0, :CHAIN], -row_offset, axis=0)
    cross_out = jnp.roll(cross[0, :CHAIN], -row_offset, axis=0)
    return diag_out, cross_out
```

```python
import functools

import jax
import jax.numpy as jnp
from jax import lax
from jax.experimental import pallas as pl
from jax.experimental.pallas import tpu as pltpu
from jax.sharding import PartitionSpec as P

MESH = pl.DeviceIdType.MESH
F32 = jnp.float32
BF16 = jnp.bfloat16
row_offset = 3
PIECES = 3


def split(value):
    high = value.astype(BF16)
    return high, (value - high.astype(F32)).astype(BF16)


def mm(a, b):
    return jnp.dot(a, b, preferred_element_type=F32)


def kernel(
    n,
    inv_ref, low_ref, up_ref,
    diag_ref, cross_ref,
    sig, wf, af, dpk, a_hi, a_lo, at_hi, at_lo, s_hi, s_lo,
    send_sem, recv_sem, pk_send, pk_recv,
):
    B = inv_ref.shape[1]
    Q = B // PIECES
    place = lax.axis_index("tm")
    t = (place + row_offset) % n
    s = jnp.int32(1)
    even = jnp.bool_(True) if (n.bit_length() - 2) % 2 == 0 else jnp.bool_(False)
    for k in range(1, n.bit_length() - 1):
        divides = t % (2**k) == 0
        s = jnp.where(divides, 2**k, s)
        even = jnp.where(divides, (n.bit_length() - 2 - k) % 2 == 0, even)
    is_zero = t == 0
    is_top = t == n // 2
    normal = jnp.logical_not(is_zero)
    has_children = jnp.logical_and(normal, s > 1)
    odd = jnp.logical_and(normal, jnp.logical_not(even))
    second = jnp.logical_and(jnp.logical_and(normal, even), jnp.logical_not(is_top))
    is_left = jnp.logical_and(t % (4 * s) == s, jnp.logical_not(is_top))
    parent = jnp.where(is_left, t + s, t - s)
    parent_left = parent % (8 * s) == 2 * s
    side = jnp.where(is_left == parent_left, 0, 1)
    half = s // 2
    g_half = jnp.where(is_left, 0, 1)

    def device(pos):
        return ((pos + (n - row_offset)) % n,)

    parent_dev = device(parent)
    child_dev = (
        device(t + jnp.where(is_left, -half, half)),
        device(t + jnp.where(is_left, half, -half)),
    )
    top_dev = (jnp.int32((n // 2 - row_offset) % n),)

    barrier = pltpu.get_barrier_semaphore()

    @pl.when(normal)
    def _():
        pl.semaphore_signal(barrier, inc=1, device_id=parent_dev, device_id_type=MESH)

    @pl.when(has_children)
    def _():
        for child in child_dev:
            pl.semaphore_signal(barrier, inc=1, device_id=child, device_id_type=MESH)

    @pl.when(is_zero)
    def _():
        pl.semaphore_signal(barrier, inc=1, device_id=top_dev, device_id_type=MESH)

    @pl.when(has_children)
    def _():
        pl.semaphore_wait(barrier, 3)

    @pl.when(jnp.logical_not(has_children))
    def _():
        pl.semaphore_wait(barrier, 1)

    def tri(i):
        return pl.ds(i * Q, Q), pl.ds(i * Q, B - i * Q)

    def to_child(c, k, src, dst, dev=None):
        return pltpu.make_async_remote_copy(
            src_ref=src, dst_ref=dst, send_sem=send_sem.at[c, k], recv_sem=recv_sem.at[k],
            device_id=child_dev[c] if dev is None else dev, device_id_type=MESH)

    def send_other(c, slot):
        for i in range(PIECES):
            to_child(c, i, sig.at[(slot, *tri(i))], sig.at[(0, *tri(i))]).start()

    def send_cross(c):
        for i in range(PIECES):
            rows = pl.ds(i * Q, Q)
            to_child(c, 3 + i, wf.at[c, rows], sig.at[1, rows]).start()

    def send_newest(c):
        for i in range(PIECES):
            to_child(c, 6 + i, sig.at[(4, *tri(i))], sig.at[(2, *tri(i))]).start()

    def recv(k):
        i = k % 3
        if k // 3 == 1:
            ref = sig.at[1, pl.ds(i * Q, Q)]
        else:
            ref = sig.at[(k // 3, *tri(i))]
        return ref, to_child(0, k, ref, ref)

    def packet(c):
        copies = []
        for i in range(2):
            copies.append((af.at[1, i], af.at[0, i]))
        for i in range(PIECES):
            copies.append((inv_ref.at[(0, *tri(i))], dpk.at[(0, *tri(i))]))
        return [
            pltpu.make_async_remote_copy(
                src_ref=src, dst_ref=dst, send_sem=pk_send.at[c, k], recv_sem=pk_recv.at[k],
                device_id=child_dev[c], device_id_type=MESH)
            for k, (src, dst) in enumerate(copies)
        ]

    def mirror(ref, slot):
        for i in range(PIECES):
            for j in range(i + 1, PIECES):
                ref[slot, j * Q:(j + 1) * Q, i * Q:(i + 1) * Q] = ref[slot, i * Q:(i + 1) * Q, j * Q:(j + 1) * Q].T

    zero_sends = [
        to_child(0, 6 + i, inv_ref.at[(0, *tri(i))], sig.at[(2, *tri(i))], dev=top_dev) for i in range(PIECES)
    ]

    @pl.when(is_zero)
    def _():
        for copy in zero_sends:
            copy.start()
        diag_ref[...] = inv_ref[...]
        cross_ref[...] = jnp.zeros_like(cross_ref)
        for copy in zero_sends:
            copy.wait_send()

    @pl.when(odd & has_children)
    def _():
        for c in range(2):
            for copy in packet(c)[2:]:
                copy.start()

    def prepare(i):
        for h in range(2):
            hi, lo = split(af[i, h])
            cols = slice(h * B, (h + 1) * B)
            a_hi[i, :, cols] = hi
            a_lo[i, :, cols] = lo
            hi_t, lo_t = split(af[i, h].T)
            at_hi[i, cols, :] = hi_t
            at_lo[i, cols, :] = lo_t

    def put_s(row, col, value):
        hi, lo = split(value)
        rows, cols = slice(row * B, (row + 1) * B), slice(col * B, (col + 1) * B)
        s_hi[rows, cols] = hi
        s_lo[rows, cols] = lo

    @pl.when(normal)
    def _():
        dpk[1] = inv_ref[0]
        d_hi, d_lo = split(inv_ref[0])
        for ref, where in ((low_ref, g_half), (up_ref, 1 - g_half)):
            hi, lo = split(ref[0])
            af[1, where] = mm(d_hi, hi) + mm(d_hi, lo) + mm(d_lo, hi)

        @pl.when(odd & has_children)
        def _():
            for c in range(2):
                for copy in packet(c)[:2]:
                    copy.start()

        prepare(1)

        @pl.when(second)
        def _():
            for copy in packet(0):
                copy.wait_recv()
            mirror(dpk, 0)
            prepare(0)

        @pl.when(is_top)
        def _():
            sig[0] = jnp.zeros((B, B), F32)
            sig[1] = jnp.zeros((B, B), F32)
            for k in range(6, 9):
                recv(k)[1].wait_recv()

        @pl.when(jnp.logical_not(is_top))
        def _():
            for k in range(9):
                ref, copy = recv(k)
                copy.wait_recv()

                @pl.when(odd & has_children)
                def _():
                    for c in range(2):
                        to_child(c, k, ref, ref).start()

        sends = even & has_children
        other_x = jnp.where(is_top, 0, 2 * side)
        other_p = jnp.where(is_top, 2, 3)

        @pl.when(sends)
        def _():
            send_other(0, other_x)

        mirror(sig, 0)
        mirror(sig, 2)
        put_s(0, 0, sig[0])
        put_s(1, 0, sig[1])
        put_s(0, 1, sig[1].T)
        put_s(1, 1, sig[2])

        def stage(i, carry):
            own = i == 1
            w = -(mm(a_hi[i], s_hi[...]) + mm(a_hi[i], s_lo[...]) + mm(a_lo[i], s_hi[...]))
            wf[0] = w[:, :B]
            wf[1] = w[:, B:]

            @pl.when(own & sends)
            def _():
                send_other(1, other_p)
                send_cross(0)
                send_cross(1)

            w_hi, w_lo = split(w)
            new = dpk[i] - (mm(w_hi, at_hi[i]) + mm(w_hi, at_lo[i]) + mm(w_lo, at_hi[i]))
            sig[3 + i] = new

            @pl.when(own & sends)
            def _():
                send_newest(0)
                send_newest(1)

            @pl.when(jnp.logical_not(own))
            def _():
                span = pl.ds(pl.multiple_of(side * B, B), B)
                for ref in (s_hi, s_lo):
                    ref[0:B, 0:B] = ref[span, span]
                put_s(1, 0, wf[side])
                put_s(0, 1, wf[side].T)
                put_s(1, 1, new)

            return carry

        lax.fori_loop(jnp.where(second, 0, 1), 2, stage, jnp.int32(0))
        diag_ref[0] = sig[4]
        cross_ref[0] = wf[g_half]

        @pl.when(has_children)
        def _():
            for c in range(2):
                for k in range(9):
                    to_child(c, k, recv(k)[0], recv(k)[0]).wait_send()

        @pl.when(odd & has_children)
        def _():
            for c in range(2):
                for copy in packet(c):
                    copy.wait_send()


def body(inv_diag, low_coupling, up_coupling):
    n = lax.axis_size("tm")
    B = inv_diag.shape[1]
    vmem = pl.BlockSpec(memory_space=pltpu.VMEM)
    block = jax.ShapeDtypeStruct(inv_diag.shape, F32)
    return pl.pallas_call(
        functools.partial(kernel, n),
        out_shape=(block, block),
        in_specs=[vmem] * 3,
        out_specs=(vmem, vmem),
        scratch_shapes=[
            pltpu.VMEM((5, B, B), F32),
            pltpu.VMEM((2, B, B), F32),
            pltpu.VMEM((2, 2, B, B), F32),
            pltpu.VMEM((2, B, B), F32),
            pltpu.VMEM((2, B, 2 * B), BF16),
            pltpu.VMEM((2, B, 2 * B), BF16),
            pltpu.VMEM((2, 2 * B, B), BF16),
            pltpu.VMEM((2, 2 * B, B), BF16),
            pltpu.VMEM((2 * B, 2 * B), BF16),
            pltpu.VMEM((2 * B, 2 * B), BF16),
            pltpu.SemaphoreType.DMA((2, 9)),
            pltpu.SemaphoreType.DMA((9,)),
            pltpu.SemaphoreType.DMA((2, 5)),
            pltpu.SemaphoreType.DMA((5,)),
        ],
        compiler_params=pltpu.CompilerParams(
            collective_id=0, has_side_effects=True, vmem_limit_bytes=60 * 1024 * 1024
        ),
    )(inv_diag, low_coupling, up_coupling)


def solution(mesh):
    placed = (P("tm", None, None),) * 3
    return jax.shard_map(
        body,
        mesh=mesh,
        in_specs=placed,
        out_specs=(P("tm", None, None), P("tm", None, None)),
        check_vma=False,
    )
```

```python
import functools

import jax
import jax.numpy as jnp
from jax import lax
from jax.experimental import pallas as pl
from jax.experimental.pallas import tpu as pltpu
from jax.sharding import PartitionSpec as P

MESH = pl.DeviceIdType.MESH
F32 = jnp.float32
BF16 = jnp.bfloat16
row_offset = 3
PIECES = 6


def split(value):
    high = value.astype(BF16)
    return high, (value - high.astype(F32)).astype(BF16)


def mm(a, b):
    return jnp.dot(a, b, preferred_element_type=F32)


def kernel(
    n,
    inv_ref, low_ref, up_ref,
    diag_ref, cross_ref,
    sig, wf, af, dpk, a_hi, a_lo, at_hi, at_lo, s_hi, s_lo,
    send_sem, recv_sem, pk_send, pk_recv,
):
    B = inv_ref.shape[1]
    Q = B // 3
    H = B // PIECES
    place = lax.axis_index("tm")
    t = (place + row_offset) % n
    s = jnp.int32(1)
    top_level = n.bit_length() - 2
    even = jnp.bool_(top_level % 2 == 0)
    for k in range(1, n.bit_length() - 1):
        divides = t % (2**k) == 0
        s = jnp.where(divides, 2**k, s)
        even = jnp.where(divides, (top_level - k) % 2 == 0, even)
    is_zero = t == 0
    is_top = t == n // 2
    normal = jnp.logical_not(is_zero)
    odd = jnp.logical_and(normal, jnp.logical_not(even))
    second = jnp.logical_and(jnp.logical_and(normal, even), jnp.logical_not(is_top))
    is_left = jnp.logical_and(t % (4 * s) == s, jnp.logical_not(is_top))
    parent = jnp.where(is_left, t + s, t - s)
    parent_left = parent % (8 * s) == 2 * s
    side = jnp.where(is_left == parent_left, 0, 1)
    half = s // 2
    g_half = jnp.where(is_left, 0, 1)
    to_x = jnp.where(is_left, -1, 1)

    first_round = jnp.logical_and(normal, s >= n // 8)
    source = jnp.logical_and(normal & even, s > 1)
    lower = jnp.logical_and(second & first_round, is_left)
    upper = jnp.logical_and(second & first_round, jnp.logical_not(is_left))
    late_second = jnp.logical_and(second, jnp.logical_not(first_round))
    late_odd = jnp.logical_and(odd, jnp.logical_not(first_round))
    near = jnp.logical_and(late_second, side == 1)
    has_next = odd | lower | near
    reach = jnp.where(is_top, half, half // 2)
    first_x = t + to_x * reach
    first_p = t - to_x * reach
    after = jnp.where(odd & first_round, t - half, jnp.where(lower, t + 2 * s, jnp.where(near, parent, t + to_x * half)))
    before = jnp.where(
        is_top, 0,
        jnp.where(odd & first_round, n // 2, jnp.where(
            upper, t - 2 * s, jnp.where(near, 2 * t - parent, jnp.where(late_odd, t - to_x * half, parent)))))
    near_child = t - to_x * half

    def device(pos):
        return ((pos + (n - row_offset)) % n,)

    ends = (device(first_x), device(first_p), device(after))
    top_dev, quarter_dev, zero_dev = device(jnp.int32(n // 2)), device(jnp.int32(n // 4)), device(jnp.int32(0))
    at_quarter = t == n // 4

    barrier = pltpu.get_barrier_semaphore()

    def greet(dev):
        pl.semaphore_signal(barrier, inc=1, device_id=dev, device_id_type=MESH)

    @pl.when(normal)
    def _():
        greet(device(before))

    @pl.when(near)
    def _():
        greet(device(parent))

    @pl.when(at_quarter)
    def _():
        greet(zero_dev)

    def number(flag):
        return jnp.where(flag, 1, 0)

    peers = 2 * number(is_zero) + 2 * number(source) + number(has_next) + number(late_odd)

    @pl.when(peers > 0)
    def _():
        pl.semaphore_wait(barrier, peers)

    def tri(i):
        start = i * H // Q * Q
        return pl.ds(i * H, H), pl.ds(start, B - start)

    def piece(slot, i, whole):
        return sig.at[slot, pl.ds(i * H, H)] if whole else sig.at[(slot, *tri(i))]

    def copy_to(e, k, src, dst, dev=None):
        return pltpu.make_async_remote_copy(
            src_ref=src, dst_ref=dst, send_sem=send_sem.at[e, k], recv_sem=recv_sem.at[k],
            device_id=ends[e] if dev is None else dev, device_id_type=MESH)

    def target(k):
        return piece(k // PIECES, k % PIECES, k // PIECES == 1)

    def send(e, part, source_of):
        for i in range(PIECES):
            k = part * PIECES + i
            copy_to(e, k, source_of(i), target(k)).start()

    def send_other(e, slot):
        send(e, 0, lambda i: piece(slot, i, False))

    def send_cross(e):
        send(e, 1, lambda i: wf.at[e, pl.ds(i * H, H)])

    def send_newest(e):
        send(e, 2, lambda i: piece(4, i, False))

    KINDS = 3 * PIECES

    def packet_parts():
        parts = [(inv_ref.at[(0, *tri(i))], dpk.at[(0, *tri(i))]) for i in range(PIECES)]
        parts += [(af.at[1, i // 2, pl.ds(i % 2 * B // 2, B // 2)], af.at[0, i // 2, pl.ds(i % 2 * B // 2, B // 2)]) for i in range(4)]
        return parts

    PARTS = PIECES + 4

    def packet(e, k, src, dst, dev):
        return pltpu.make_async_remote_copy(
            src_ref=src, dst_ref=dst, send_sem=pk_send.at[e, k], recv_sem=pk_recv.at[k],
            device_id=dev, device_id_type=MESH)

    def send_packet(chosen):
        for k in chosen:
            src, dst = packet_parts()[k]
            packet(0, k, src, dst, ends[2]).start()

            @pl.when(late_odd)
            def _():
                packet(1, k, src, dst, device(near_child)).start()

    def mirror(ref, slot):
        for i in range(3):
            for j in range(i + 1, 3):
                ref[slot, j * Q:(j + 1) * Q, i * Q:(i + 1) * Q] = ref[slot, i * Q:(i + 1) * Q, j * Q:(j + 1) * Q].T

    def zero_sends():
        out = []
        for i in range(PIECES):
            src = inv_ref.at[(0, *tri(i))]
            out.append(copy_to(0, 2 * PIECES + i, src, target(2 * PIECES + i), top_dev))
        for i in range(PIECES):
            src = inv_ref.at[(0, *tri(i))]
            out.append(copy_to(1, i, src, target(i), quarter_dev))
        return out

    @pl.when(is_zero)
    def _():
        for copy in zero_sends():
            copy.start()
        diag_ref[...] = inv_ref[...]
        cross_ref[...] = jnp.zeros_like(cross_ref)
        for copy in zero_sends():
            copy.wait_send()

    @pl.when(odd)
    def _():
        send_packet(range(PIECES))

    @pl.when(is_top)
    def _():
        sig[0] = jnp.zeros((B, B), F32)
        sig[1] = jnp.zeros((B, B), F32)
        send_other(0, 0)
        send(0, 1, lambda i: piece(1, i, True))

    def prepare(i):
        for h in range(2):
            hi, lo = split(af[i, h])
            cols = slice(h * B, (h + 1) * B)
            a_hi[i, :, cols] = hi
            a_lo[i, :, cols] = lo
            hi_t, lo_t = split(af[i, h].T)
            at_hi[i, cols, :] = hi_t
            at_lo[i, cols, :] = lo_t

    def put_s(row, col, value):
        hi, lo = split(value)
        rows, cols = slice(row * B, (row + 1) * B), slice(col * B, (col + 1) * B)
        s_hi[rows, cols] = hi
        s_lo[rows, cols] = lo

    @pl.when(normal)
    def _():
        dpk[1] = inv_ref[0]
        d_hi, d_lo = split(inv_ref[0])
        for ref, where in ((low_ref, g_half), (up_ref, 1 - g_half)):
            hi, lo = split(ref[0])
            af[1, where] = mm(d_hi, hi) + mm(d_hi, lo) + mm(d_lo, hi)

        @pl.when(odd)
        def _():
            send_packet(range(PIECES, PARTS))

        prepare(1)

        @pl.when(second)
        def _():
            for k, (_, dst) in enumerate(packet_parts()):
                packet(0, k, dst, dst, ends[2]).wait_recv()

                @pl.when(lower)
                def _():
                    packet(0, k, dst, dst, ends[2]).start()

            mirror(dpk, 0)
            prepare(0)

        @pl.when(is_top)
        def _():
            for k in range(2 * PIECES, KINDS):
                copy_to(2, k, target(k), target(k)).wait_recv()

        @pl.when(jnp.logical_not(is_top))
        def _():
            for k in range(KINDS):
                copy_to(2, k, target(k), target(k)).wait_recv()

                @pl.when(has_next)
                def _():
                    copy_to(2, k, target(k), target(k)).start()

        sends = source

        @pl.when(sends & jnp.logical_not(is_top))
        def _():
            send_other(0, 2 * side)

        mirror(sig, 0)
        mirror(sig, 2)
        put_s(0, 0, sig[0])
        put_s(1, 0, sig[1])
        put_s(0, 1, sig[1].T)
        put_s(1, 1, sig[2])

        def stage(i, carry):
            own = i == 1
            w = -(mm(a_hi[i], s_hi[...]) + mm(a_hi[i], s_lo[...]) + mm(a_lo[i], s_hi[...]))
            wf[0] = w[:, :B]
            wf[1] = w[:, B:]

            @pl.when(own & sends)
            def _():
                @pl.when(jnp.logical_not(is_top))
                def _():
                    send_other(1, 3)
                    send_cross(0)

                send_cross(1)

            w_hi, w_lo = split(w)
            new = dpk[i] - (mm(w_hi, at_hi[i]) + mm(w_hi, at_lo[i]) + mm(w_lo, at_hi[i]))
            sig[3 + i] = new

            @pl.when(own & sends)
            def _():
                send_newest(0)
                send_newest(1)

            @pl.when(jnp.logical_not(own))
            def _():
                span = pl.ds(pl.multiple_of(side * B, B), B)
                for ref in (s_hi, s_lo):
                    ref[0:B, 0:B] = ref[span, span]
                put_s(1, 0, wf[side])
                put_s(0, 1, wf[side].T)
                put_s(1, 1, new)

            return carry

        lax.fori_loop(jnp.where(second, 0, 1), 2, stage, jnp.int32(0))
        diag_ref[0] = sig[4]
        cross_ref[0] = wf[g_half]

        def drain(e, kinds):
            for k in kinds:
                copy_to(e, k, target(k), target(k)).wait_send()

        @pl.when(source)
        def _():
            drain(0, range(KINDS))
            drain(1, range(PIECES, KINDS))

        @pl.when(source & jnp.logical_not(is_top))
        def _():
            drain(1, range(PIECES))

        @pl.when(has_next)
        def _():
            drain(2, range(KINDS))

        def drain_packet(e):
            for k, (src, dst) in enumerate(packet_parts()):
                packet(e, k, src, dst, ends[2]).wait_send()

        @pl.when(odd | lower)
        def _():
            drain_packet(0)

        @pl.when(late_odd)
        def _():
            drain_packet(1)


def body(inv_diag, low_coupling, up_coupling):
    n = lax.axis_size("tm")
    B = inv_diag.shape[1]
    vmem = pl.BlockSpec(memory_space=pltpu.VMEM)
    block = jax.ShapeDtypeStruct(inv_diag.shape, F32)
    return pl.pallas_call(
        functools.partial(kernel, n),
        out_shape=(block, block),
        in_specs=[vmem] * 3,
        out_specs=(vmem, vmem),
        scratch_shapes=[
            pltpu.VMEM((5, B, B), F32),
            pltpu.VMEM((2, B, B), F32),
            pltpu.VMEM((2, 2, B, B), F32),
            pltpu.VMEM((2, B, B), F32),
            pltpu.VMEM((2, B, 2 * B), BF16),
            pltpu.VMEM((2, B, 2 * B), BF16),
            pltpu.VMEM((2, 2 * B, B), BF16),
            pltpu.VMEM((2, 2 * B, B), BF16),
            pltpu.VMEM((2 * B, 2 * B), BF16),
            pltpu.VMEM((2 * B, 2 * B), BF16),
            pltpu.SemaphoreType.DMA((3, 3 * PIECES)),
            pltpu.SemaphoreType.DMA((3 * PIECES,)),
            pltpu.SemaphoreType.DMA((2, PIECES + 4)),
            pltpu.SemaphoreType.DMA((PIECES + 4,)),
        ],
        compiler_params=pltpu.CompilerParams(
            collective_id=0, has_side_effects=True, vmem_limit_bytes=60 * 1024 * 1024
        ),
    )(inv_diag, low_coupling, up_coupling)


def solution(mesh):
    placed = (P("tm", None, None),) * 3
    return jax.shard_map(
        body,
        mesh=mesh,
        in_specs=placed,
        out_specs=(P("tm", None, None), P("tm", None, None)),
        check_vma=False,
    )
```

```python
import functools

import jax
import jax.numpy as jnp
from jax import lax
from jax.experimental import pallas as pl
from jax.experimental.pallas import tpu as pltpu
from jax.sharding import PartitionSpec as P

MESH = pl.DeviceIdType.MESH
F32 = jnp.float32
BF16 = jnp.bfloat16
row_offset = 3
PIECES = 6


def split(value):
    high = value.astype(BF16)
    return high, (value - high.astype(F32)).astype(BF16)


def mm(a, b):
    return jnp.dot(a, b, preferred_element_type=F32)


def kernel(
    n,
    inv_ref, low_ref, up_ref,
    diag_ref, cross_ref,
    sig, wf, af, dpk, a_hi, a_lo, at_hi, at_lo, s_hi, s_lo,
    send_sem, recv_sem, pk_send, pk_recv, go_sem,
):
    B = inv_ref.shape[1]
    Q = B // 3
    H = B // PIECES
    place = lax.axis_index("tm")
    t = (place + row_offset) % n
    s = jnp.int32(1)
    top_level = n.bit_length() - 2
    even = jnp.bool_(top_level % 2 == 0)
    for k in range(1, n.bit_length() - 1):
        divides = t % (2**k) == 0
        s = jnp.where(divides, 2**k, s)
        even = jnp.where(divides, (top_level - k) % 2 == 0, even)
    is_zero = t == 0
    is_top = t == n // 2
    normal = jnp.logical_not(is_zero)
    odd = jnp.logical_and(normal, jnp.logical_not(even))
    second = jnp.logical_and(jnp.logical_and(normal, even), jnp.logical_not(is_top))
    is_left = jnp.logical_and(t % (4 * s) == s, jnp.logical_not(is_top))
    parent = jnp.where(is_left, t + s, t - s)
    parent_left = parent % (8 * s) == 2 * s
    side = jnp.where(is_left == parent_left, 0, 1)
    half = s // 2
    g_half = jnp.where(is_left, 0, 1)
    to_x = jnp.where(is_left, -1, 1)

    first_round = jnp.logical_and(normal, s >= n // 8)
    source = jnp.logical_and(normal & even, s > 1)
    right = first_round & (t > n // 2)
    lower = jnp.logical_and(second & first_round, is_left)
    late_odd = jnp.logical_and(odd, jnp.logical_not(first_round))
    near = jnp.logical_and(second, side == 1)
    has_next = (second & jnp.logical_not(right)) | (right & (t < 7 * n // 8))
    first_x = t + to_x * jnp.where(is_top, half, half // 2)
    first_p = t - to_x * (half // 2)
    after = jnp.where(right, jnp.where(odd, t - half, t + n // 4), jnp.where(near, 2 * parent - t, parent))
    before = jnp.where(
        is_top, 0,
        jnp.where(right, jnp.where(odd, n // 2, jnp.where(lower, parent, t - n // 4)), jnp.where(
            near, 2 * t - parent, jnp.where(odd, t + to_x * half, 2 * parent - t))))
    packet_from = jnp.where(first_round & jnp.logical_not(lower), t - n // 4, parent)
    packet_to = jnp.where(odd & first_round, t - half, jnp.where(lower, t + n // 4, t + to_x * half))
    near_child = t - to_x * half
    held = normal & is_left & (s == n // 16)
    holder = normal & (s == n // 8)

    def device(pos):
        return ((pos + (n - row_offset)) % n,)

    ends = (device(first_x), device(first_p), device(after))
    top_dev, start_dev, zero_dev = device(jnp.int32(n // 2)), device(jnp.int32(3 * n // 8)), device(jnp.int32(0))
    at_start = t == 3 * n // 8
    held_dev = device(t - n // 16)

    barrier = pltpu.get_barrier_semaphore()

    def greet(dev):
        pl.semaphore_signal(barrier, inc=1, device_id=dev, device_id_type=MESH)

    @pl.when(normal)
    def _():
        greet(device(before))

    @pl.when(second)
    def _():
        greet(device(packet_from))

    @pl.when(at_start)
    def _():
        greet(zero_dev)

    @pl.when(held)
    def _():
        greet(device(parent))

    def number(flag):
        return jnp.where(flag, 1, 0)

    peers = (
        2 * number(is_zero) + 2 * number(source) + number(has_next) + 2 * number(late_odd)
        + number(odd & first_round) + number(lower) + (number(holder) if n >= 32 else 0))

    @pl.when(peers > 0)
    def _():
        pl.semaphore_wait(barrier, peers)

    def tri(i):
        start = i * H // Q * Q
        return pl.ds(i * H, H), pl.ds(start, B - start)

    def piece(slot, i, whole):
        return sig.at[slot, pl.ds(i * H, H)] if whole else sig.at[(slot, *tri(i))]

    def copy_to(e, k, src, dst, dev=None):
        return pltpu.make_async_remote_copy(
            src_ref=src, dst_ref=dst, send_sem=send_sem.at[e, k], recv_sem=recv_sem.at[k],
            device_id=ends[e] if dev is None else dev, device_id_type=MESH)

    def target(k):
        return piece(k // PIECES, k % PIECES, k // PIECES == 1)

    def send(e, part, source_of):
        for i in range(PIECES):
            k = part * PIECES + i
            copy_to(e, k, source_of(i), target(k)).start()

    def send_other(e, slot):
        send(e, 0, lambda i: piece(slot, i, False))

    def send_cross(e):
        send(e, 1, lambda i: wf.at[e, pl.ds(i * H, H)])

    def send_newest(e):
        send(e, 2, lambda i: piece(4, i, False))

    KINDS = 3 * PIECES

    def packet_parts():
        parts = [(inv_ref.at[(0, *tri(i))], dpk.at[(0, *tri(i))]) for i in range(PIECES)]
        parts += [(af.at[1, i // 2, pl.ds(i % 2 * B // 2, B // 2)], af.at[0, i // 2, pl.ds(i % 2 * B // 2, B // 2)]) for i in range(4)]
        return parts

    PARTS = PIECES + 4

    def packet(e, k, src, dst, dev):
        return pltpu.make_async_remote_copy(
            src_ref=src, dst_ref=dst, send_sem=pk_send.at[e, k], recv_sem=pk_recv.at[k],
            device_id=dev, device_id_type=MESH)

    def send_packet(e, chosen, dev):
        for k in chosen:
            src, dst = packet_parts()[k]
            packet(e, k, src, dst, dev).start()

    def mirror(ref, slot):
        for i in range(3):
            for j in range(i + 1, 3):
                ref[slot, j * Q:(j + 1) * Q, i * Q:(i + 1) * Q] = ref[slot, i * Q:(i + 1) * Q, j * Q:(j + 1) * Q].T

    def zero_sends():
        out = []
        for i in range(PIECES):
            src = inv_ref.at[(0, *tri(i))]
            out.append(copy_to(0, 2 * PIECES + i, src, target(2 * PIECES + i), top_dev))
        for i in range(PIECES):
            src = inv_ref.at[(0, *tri(i))]
            out.append(copy_to(1, i, src, target(i), start_dev))
        return out

    @pl.when(is_zero)
    def _():
        for copy in zero_sends():
            copy.start()
        diag_ref[...] = inv_ref[...]
        cross_ref[...] = jnp.zeros_like(cross_ref)
        for copy in zero_sends():
            copy.wait_send()

    early = late_odd & jnp.logical_not(held)

    @pl.when(odd)
    def _():
        send_packet(0, range(PIECES), device(packet_to))

    @pl.when(early)
    def _():
        send_packet(1, range(PIECES), device(near_child))

    @pl.when(is_top | right)
    def _():
        sig[0] = jnp.zeros((B, B), F32)
        sig[1] = jnp.zeros((B, B), F32)

    def prepare(i):
        for h in range(2):
            hi, lo = split(af[i, h])
            cols = slice(h * B, (h + 1) * B)
            a_hi[i, :, cols] = hi
            a_lo[i, :, cols] = lo
            hi_t, lo_t = split(af[i, h].T)
            at_hi[i, cols, :] = hi_t
            at_lo[i, cols, :] = lo_t

    def put_s(row, col, value):
        hi, lo = split(value)
        rows, cols = slice(row * B, (row + 1) * B), slice(col * B, (col + 1) * B)
        s_hi[rows, cols] = hi
        s_lo[rows, cols] = lo

    @pl.when(normal)
    def _():
        dpk[1] = inv_ref[0]
        d_hi, d_lo = split(inv_ref[0])
        for ref, where in ((low_ref, g_half), (up_ref, 1 - g_half)):
            hi, lo = split(ref[0])
            af[1, where] = mm(d_hi, hi) + mm(d_hi, lo) + mm(d_lo, hi)

        @pl.when(odd)
        def _():
            send_packet(0, range(PIECES, PARTS), device(packet_to))

        @pl.when(early)
        def _():
            send_packet(1, range(PIECES, PARTS), device(near_child))

        prepare(1)

        if n >= 32:
            @pl.when(held)
            def _():
                pl.semaphore_wait(go_sem, 1)
                send_packet(1, range(PARTS), device(near_child))

        @pl.when(second)
        def _():
            for k, (_, dst) in enumerate(packet_parts()):
                packet(0, k, dst, dst, zero_dev).wait_recv()

                @pl.when(lower)
                def _():
                    packet(0, k, dst, dst, device(packet_to)).start()

            mirror(dpk, 0)
            prepare(0)

        def receive(kinds):
            for k in kinds:
                copy_to(2, k, target(k), target(k)).wait_recv()

                @pl.when(has_next)
                def _():
                    copy_to(2, k, target(k), target(k)).start()

        @pl.when(jnp.logical_not(is_top | right))
        def _():
            receive(range(2 * PIECES))

        receive(range(2 * PIECES, KINDS))

        if n >= 32:
            @pl.when(holder)
            def _():
                pl.semaphore_signal(go_sem, inc=1, device_id=held_dev, device_id_type=MESH)

        sends = source

        @pl.when(sends & jnp.logical_not(is_top))
        def _():
            send_other(0, 2 * side)

        mirror(sig, 0)
        mirror(sig, 2)
        put_s(0, 0, sig[0])
        put_s(1, 0, sig[1])
        put_s(0, 1, sig[1].T)
        put_s(1, 1, sig[2])

        def stage(i, carry):
            own = i == 1
            w = -(mm(a_hi[i], s_hi[...]) + mm(a_hi[i], s_lo[...]) + mm(a_lo[i], s_hi[...]))
            wf[0] = w[:, :B]
            wf[1] = w[:, B:]

            @pl.when(own & sends)
            def _():
                @pl.when(jnp.logical_not(is_top))
                def _():
                    send_cross(0)

                send_cross(1)

            w_hi, w_lo = split(w)
            new = dpk[i] - (mm(w_hi, at_hi[i]) + mm(w_hi, at_lo[i]) + mm(w_lo, at_hi[i]))
            sig[3 + i] = new

            @pl.when(own & sends)
            def _():
                send_newest(0)
                send_newest(1)

            @pl.when(jnp.logical_not(own) & sends)
            def _():
                send_other(1, 3)

            @pl.when(jnp.logical_not(own))
            def _():
                span = pl.ds(pl.multiple_of(side * B, B), B)
                for ref in (s_hi, s_lo):
                    ref[0:B, 0:B] = ref[span, span]
                put_s(1, 0, wf[side])
                put_s(0, 1, wf[side].T)
                put_s(1, 1, new)

            return carry

        lax.fori_loop(jnp.where(second, 0, 1), 2, stage, jnp.int32(0))
        diag_ref[0] = sig[4]
        cross_ref[0] = wf[g_half]

        def drain(e, kinds):
            for k in kinds:
                copy_to(e, k, target(k), target(k)).wait_send()

        @pl.when(source)
        def _():
            drain(0, range(2 * PIECES, KINDS))
            drain(1, range(PIECES, KINDS))

        @pl.when(source & jnp.logical_not(is_top))
        def _():
            drain(0, range(2 * PIECES))
            drain(1, range(PIECES))

        @pl.when(has_next)
        def _():
            drain(2, range(2 * PIECES, KINDS))

        @pl.when(has_next & jnp.logical_not(right))
        def _():
            drain(2, range(2 * PIECES))

        def drain_packet(e):
            for k, (src, dst) in enumerate(packet_parts()):
                packet(e, k, src, dst, zero_dev).wait_send()

        @pl.when(odd | lower)
        def _():
            drain_packet(0)

        @pl.when(late_odd)
        def _():
            drain_packet(1)


def body(inv_diag, low_coupling, up_coupling):
    n = lax.axis_size("tm")
    B = inv_diag.shape[1]
    vmem = pl.BlockSpec(memory_space=pltpu.VMEM)
    block = jax.ShapeDtypeStruct(inv_diag.shape, F32)
    return pl.pallas_call(
        functools.partial(kernel, n),
        out_shape=(block, block),
        in_specs=[vmem] * 3,
        out_specs=(vmem, vmem),
        scratch_shapes=[
            pltpu.VMEM((5, B, B), F32),
            pltpu.VMEM((2, B, B), F32),
            pltpu.VMEM((2, 2, B, B), F32),
            pltpu.VMEM((2, B, B), F32),
            pltpu.VMEM((2, B, 2 * B), BF16),
            pltpu.VMEM((2, B, 2 * B), BF16),
            pltpu.VMEM((2, 2 * B, B), BF16),
            pltpu.VMEM((2, 2 * B, B), BF16),
            pltpu.VMEM((2 * B, 2 * B), BF16),
            pltpu.VMEM((2 * B, 2 * B), BF16),
            pltpu.SemaphoreType.DMA((3, 3 * PIECES)),
            pltpu.SemaphoreType.DMA((3 * PIECES,)),
            pltpu.SemaphoreType.DMA((2, PIECES + 4)),
            pltpu.SemaphoreType.DMA((PIECES + 4,)),
            pltpu.SemaphoreType.REGULAR,
        ],
        compiler_params=pltpu.CompilerParams(
            collective_id=0, has_side_effects=True, vmem_limit_bytes=60 * 1024 * 1024
        ),
    )(inv_diag, low_coupling, up_coupling)


def solution(mesh):
    placed = (P("tm", None, None),) * 3
    return jax.shard_map(
        body,
        mesh=mesh,
        in_specs=placed,
        out_specs=(P("tm", None, None), P("tm", None, None)),
        check_vma=False,
    )
```

```python
import functools

import jax
import jax.numpy as jnp
from jax import lax
from jax.experimental import pallas as pl
from jax.experimental.pallas import tpu as pltpu
from jax.sharding import PartitionSpec as P

MESH = pl.DeviceIdType.MESH
F32 = jnp.float32
BF16 = jnp.bfloat16
row_offset = 3
PIECES = 6


def split(value):
    high = value.astype(BF16)
    return high, (value - high.astype(F32)).astype(BF16)


def mm(a, b):
    return jnp.dot(a, b, preferred_element_type=F32)


def kernel(
    n,
    inv_ref, low_ref, up_ref,
    diag_ref, cross_ref,
    sig, wf, tmp, af, dpk, a_hi, a_lo, at_hi, at_lo, s_hi, s_lo,
    send_sem, recv_sem, pk_send, pk_recv, res_send, res_recv, go_sem, call_sem,
):
    B = inv_ref.shape[1]
    Q = B // 3
    H = B // PIECES
    place = lax.axis_index("tm")
    t = (place + row_offset) % n
    s = jnp.int32(1)
    top_level = n.bit_length() - 2
    even = jnp.bool_(top_level % 2 == 0)
    for k in range(1, n.bit_length() - 1):
        divides = t % (2**k) == 0
        s = jnp.where(divides, 2**k, s)
        even = jnp.where(divides, (top_level - k) % 2 == 0, even)
    is_zero = t == 0
    is_top = t == n // 2
    normal = jnp.logical_not(is_zero)
    odd = jnp.logical_and(normal, jnp.logical_not(even))
    second = jnp.logical_and(jnp.logical_and(normal, even), jnp.logical_not(is_top))
    is_left = jnp.logical_and(t % (4 * s) == s, jnp.logical_not(is_top))
    parent = jnp.where(is_left, t + s, t - s)
    parent_left = parent % (8 * s) == 2 * s
    side = jnp.where(is_left == parent_left, 0, 1)
    half = s // 2
    g_half = jnp.where(is_left, 0, 1)
    to_x = jnp.where(is_left, -1, 1)

    first_round = jnp.logical_and(normal, s >= n // 8)
    source = jnp.logical_and(normal & even, s > 1)
    right = first_round & (t > n // 2)
    lower = jnp.logical_and(second & first_round, is_left)
    late_odd = jnp.logical_and(odd, jnp.logical_not(first_round))
    near = jnp.logical_and(second, side == 1)
    has_next = (near & jnp.logical_not(right)) | (right & (t < 7 * n // 8))
    first_x = t + to_x * jnp.where(is_top, half, half // 2)
    first_p = t - to_x * (half // 2)
    after = jnp.where(right, jnp.where(odd, t - half, t + n // 4), 2 * parent - t)
    before = jnp.where(
        is_top, 0,
        jnp.where(right, jnp.where(odd, n // 2, jnp.where(lower, parent, t - n // 4)), jnp.where(
            near, 2 * t - parent, 2 * parent - t)))
    packet_from = jnp.where(first_round & jnp.logical_not(lower), t - n // 4, parent)
    packet_to = jnp.where(odd & first_round, t - half, jnp.where(lower, t + n // 4, t + to_x * half))
    near_child = t - to_x * half
    feeds_cross = second & is_left
    feeds_sigma = second & (is_left == (s == 1))
    last_odd = odd & (s == 2)
    held = normal & is_left & (s == n // 16) & (t < 3 * n // 4)
    half_held = t == 5 * n // 16
    calls = held & jnp.logical_not(half_held)
    at_start = t == 3 * n // 8
    late_packet = (near & parent_left & (2 * s == n // 16) & (t < 3 * n // 4)) | at_start
    holder = lower | at_start

    bends = n >= 128
    hub = (t % 32 == 10) & bends
    bend_p = near & jnp.logical_not(is_left | first_round) & (s == 4) & bends
    bend_x = second & is_left & jnp.logical_not(near | first_round) & (s == 4) & bends
    bend_q = (s == 16) & normal & bends
    first_x = first_x - jnp.where(bend_q & is_left, 2, 0)
    first_p = first_p - jnp.where(bend_q & jnp.logical_not(is_left), 2, 0)
    before = jnp.where(hub, t + 6, jnp.where(bend_p, t - 2, jnp.where(bend_x, t + 6, before)))
    has_next = has_next & jnp.logical_not(bend_p)
    after = jnp.where(hub, t + 2, after)
    forwards = has_next & jnp.logical_not(late_packet)

    def device(pos):
        return ((pos + (n - row_offset)) % n,)

    ends = (device(first_x), device(first_p), device(after))
    top_dev, start_dev, zero_dev = device(jnp.int32(n // 2)), device(jnp.int32(3 * n // 8)), device(jnp.int32(0))
    held_dev = device(t - n // 16)

    barrier = pltpu.get_barrier_semaphore()

    def greet(dev):
        pl.semaphore_signal(barrier, inc=1, device_id=dev, device_id_type=MESH)

    @pl.when((normal & even) | right | hub)
    def _():
        greet(device(before))

    @pl.when(odd)
    def _():
        greet(device(t - half))

        @pl.when(jnp.logical_not(last_odd))
        def _():
            greet(device(t + half))

    if n >= 32:
        @pl.when(lower)
        def _():
            greet(held_dev)

    @pl.when(second)
    def _():
        greet(device(packet_from))

    @pl.when(at_start)
    def _():
        greet(zero_dev)

    @pl.when(held)
    def _():
        greet(device(parent))

    def number(flag):
        return jnp.where(flag, 1, 0)

    peers = (
        2 * number(is_zero) + 2 * number(source) + number(has_next) + 2 * number(late_odd)
        + number(odd & first_round) + number(lower) + number(feeds_cross) + number(feeds_sigma & (s > 1)) + (number(holder) + number(calls) if n >= 32 else 0) + 2 * number(hub))

    @pl.when(peers > 0)
    def _():
        pl.semaphore_wait(barrier, peers)

    def tri(i):
        start = i * H // Q * Q
        return pl.ds(i * H, H), pl.ds(start, B - start)

    def piece(slot, i, whole):
        return sig.at[slot, pl.ds(i * H, H)] if whole else sig.at[(slot, *tri(i))]

    def copy_to(e, k, src, dst, dev=None):
        return pltpu.make_async_remote_copy(
            src_ref=src, dst_ref=dst, send_sem=send_sem.at[e, k], recv_sem=recv_sem.at[k],
            device_id=ends[e] if dev is None else dev, device_id_type=MESH)

    def target(k):
        return piece(k // PIECES, k % PIECES, k // PIECES == 1)

    def send(e, part, source_of):
        for i in range(PIECES):
            k = part * PIECES + i
            copy_to(e, k, source_of(i), target(k)).start()

    def send_other(e, slot):
        send(e, 0, lambda i: piece(slot, i, False))

    def send_cross(e):
        send(e, 1, lambda i: wf.at[1, e, pl.ds(i * H, H)])

    def send_newest(e):
        send(e, 2, lambda i: piece(4, i, False))

    KINDS = 3 * PIECES

    def packet_parts():
        parts = [(inv_ref.at[(0, *tri(i))], dpk.at[(0, *tri(i))]) for i in range(PIECES)]
        parts += [(af.at[1, i // 3, pl.ds(i % 3 * Q, Q)], af.at[0, i // 3, pl.ds(i % 3 * Q, Q)]) for i in range(6)]
        return parts

    PARTS = PIECES + 6

    def packet(e, k, src, dst, dev):
        return pltpu.make_async_remote_copy(
            src_ref=src, dst_ref=dst, send_sem=pk_send.at[e, k], recv_sem=pk_recv.at[k],
            device_id=dev, device_id_type=MESH)

    def send_packet(e, chosen, dev):
        for k in chosen:
            src, dst = packet_parts()[k]
            packet(e, k, src, dst, dev).start()

    def mirror(ref, slot):
        for i in range(3):
            for j in range(i + 1, 3):
                ref[slot, j * Q:(j + 1) * Q, i * Q:(i + 1) * Q] = ref[slot, i * Q:(i + 1) * Q, j * Q:(j + 1) * Q].T

    def zero_sends():
        out = []
        for i in range(PIECES):
            src = inv_ref.at[(0, *tri(i))]
            out.append(copy_to(0, 2 * PIECES + i, src, target(2 * PIECES + i), top_dev))
        for i in range(PIECES):
            src = inv_ref.at[(0, *tri(i))]
            out.append(copy_to(1, i, src, target(i), start_dev))
        return out

    @pl.when(is_zero)
    def _():
        for copy in zero_sends():
            copy.start()
        diag_ref[...] = inv_ref[...]
        cross_ref[...] = jnp.zeros_like(cross_ref)
        for copy in zero_sends():
            copy.wait_send()

    early = late_odd & jnp.logical_not(held)

    @pl.when(odd)
    def _():
        send_packet(0, range(PIECES), device(packet_to))

    @pl.when(early)
    def _():
        send_packet(1, range(PIECES), device(near_child))

    @pl.when(is_top | right)
    def _():
        sig[0] = jnp.zeros((B, B), F32)
        sig[1] = jnp.zeros((B, B), F32)

    def prepare(i):
        for h in range(2):
            hi, lo = split(af[i, h])
            a_hi[i, :, part(h)] = hi
            a_lo[i, :, part(h)] = lo
            hi_t, lo_t = split(af[i, h].T)
            at_hi[i, part(h), :] = hi_t
            at_lo[i, part(h), :] = lo_t

    def part(h):
        return slice(h * B, (h + 1) * B)

    def put_s(i, row, col, value):
        s_hi[i, part(row), part(col)], s_lo[i, part(row), part(col)] = split(value)

    def three(a, b):
        return mm(a[0], b[0]) + mm(a[0], b[1]) + mm(a[1], b[0])

    def coeff(i, h):
        return a_hi[i, :, part(h)], a_lo[i, :, part(h)]

    def coeff_t(i, h):
        return at_hi[i, part(h), :], at_lo[i, part(h), :]

    def held_s(i, row, col):
        return s_hi[i, part(row), part(col)], s_lo[i, part(row), part(col)]

    def cross_old(i):
        whole = (a_hi[i], a_lo[i])
        wf[i, 0] = -three(whole, (s_hi[i, :, part(0)], s_lo[i, :, part(0)]))

    def partial_new(i):
        tmp[i, 0] = three(coeff(i, 0), held_s(i, 0, 1))

    def partial_sum(i):
        tmp[i, 1] = dpk[i] - three(split(wf[i, 0]), coeff_t(i, 0))

    def cross_new(i):
        wf[i, 1] = -(tmp[i, 0] + three(coeff(i, 1), held_s(i, 1, 1)))

    def newest(i):
        sig[3 + i] = tmp[i, 1] - three(split(wf[i, 1]), coeff_t(i, 1))

    def result(k, src, dst):
        return pltpu.make_async_remote_copy(
            src_ref=src, dst_ref=dst, send_sem=res_send.at[k], recv_sem=res_recv.at[k],
            device_id=device(parent), device_id_type=MESH)

    def sigma_result():
        return [result(i, sig.at[(3, *tri(i))], sig.at[(4, *tri(i))]) for i in range(PIECES)]

    def cross_result():
        own = jnp.where(parent_left, 0, 1)
        return [
            result(PIECES + i, wf.at[0, own, pl.ds(i * Q, Q)], wf.at[1, 0, pl.ds(i * Q, Q)]) for i in range(3)
        ]

    def receive(kinds):
        for k in kinds:
            copy_to(2, k, target(k), target(k)).wait_recv()

            @pl.when(has_next)
            def _():
                copy_to(2, k, target(k), target(k)).start()

    def drain(e, kinds):
        for k in kinds:
            copy_to(e, k, target(k), target(k)).wait_send()

    def drain_packet(e):
        for k, (src, dst) in enumerate(packet_parts()):
            packet(e, k, src, dst, zero_dev).wait_send()

    LAST = range(2 * PIECES, KINDS)

    @pl.when(normal)
    def _():
        dpk[1] = inv_ref[0]
        inverse = split(inv_ref[0])
        for ref, where in ((low_ref, g_half), (up_ref, 1 - g_half)):
            af[1, where] = three(inverse, split(ref[0]))

    @pl.when(odd)
    def _():
        send_packet(0, range(PIECES, PARTS), device(packet_to))

        @pl.when(early)
        def _():
            send_packet(1, range(PIECES, PARTS), device(near_child))

        if n >= 32:
            @pl.when(half_held)
            def _():
                send_packet(1, range(PIECES + 3), device(near_child))

            @pl.when(held)
            def _():
                pl.semaphore_wait(go_sem, 1)

            @pl.when(held & jnp.logical_not(half_held))
            def _():
                send_packet(1, range(PIECES + 3), device(near_child))

            @pl.when(held)
            def _():
                send_packet(1, range(PIECES + 3, PARTS), device(near_child))

        @pl.when(right)
        def _():
            receive(LAST)

        @pl.when(hub)
        def _():
            for k in range(KINDS):
                copy_to(2, k, target(k), target(k)).wait_recv()
                copy_to(2, k, target(k), target(k)).start()
                copy_to(0, k, target(k), target(k), device(t - 6)).start()
            drain(2, range(KINDS))
            drain(0, range(KINDS))

        for copy in sigma_result() + cross_result():
            copy.wait_recv()

        if n >= 32:
            @pl.when(calls)
            def _():
                pl.semaphore_signal(call_sem, inc=1, device_id=device(parent), device_id_type=MESH)

        mirror(sig, 4)
        diag_ref[0] = sig[4]
        cross_ref[0] = wf[1, 0]
        drain_packet(0)

        @pl.when(late_odd)
        def _():
            drain_packet(1)

    @pl.when(is_top)
    def _():
        prepare(1)
        receive(LAST)
        mirror(sig, 2)
        put_s(1, 1, 1, sig[2])
        wf[1, 0] = jnp.zeros((B, B), F32)
        tmp[1, 0] = jnp.zeros((B, B), F32)
        tmp[1, 1] = inv_ref[0]
        cross_new(1)
        send_cross(1)
        newest(1)
        send_newest(0)
        send_newest(1)

    @pl.when(second)
    def _():
        prepare(1)

        def get_packet():
            for k, (_, dst) in enumerate(packet_parts()):
                packet(0, k, dst, dst, zero_dev).wait_recv()

                @pl.when(lower)
                def _():
                    packet(0, k, dst, dst, device(packet_to)).start()

            mirror(dpk, 0)
            prepare(0)

        def go():
            pl.semaphore_signal(go_sem, inc=1, device_id=held_dev, device_id_type=MESH)

        @pl.when(jnp.logical_not(late_packet))
        def _():
            get_packet()

        if n >= 32:
            @pl.when(lower)
            def _():
                go()

        @pl.when(jnp.logical_not(right))
        def _():
            receive(range(2 * PIECES))

        @pl.when(late_packet)
        def _():
            receive(LAST)

            if n >= 32:
                @pl.when(at_start)
                def _():
                    go()

            get_packet()

        def pass_on(kinds):
            @pl.when(forwards)
            def _():
                receive(kinds)

        @pl.when(source & (side == 0))
        def _():
            send_other(0, 0)

        mirror(sig, 0)
        put_s(0, 0, 0, sig[0])
        put_s(0, 1, 0, sig[1])
        put_s(0, 0, 1, sig[1].T)
        pass_on(LAST[:1])
        cross_old(0)
        pass_on(LAST[1:2])
        partial_new(0)
        pass_on(LAST[2:3])
        partial_sum(0)

        def own_early(block):
            s_hi[1, part(0), part(0)], s_lo[1, part(0), part(0)] = held_s(0, block, block)
            put_s(1, 1, 0, wf[0, block])
            put_s(1, 0, 1, wf[0, block].T)
            cross_old(1)

            @pl.when(source)
            def _():
                send_cross(0)

            partial_new(1)
            partial_sum(1)

        @pl.when(side == 0)
        def _():
            own_early(0)

        pass_on(LAST[3:])

        @pl.when(jnp.logical_not(forwards | late_packet))
        def _():
            receive(LAST)

        @pl.when(source & (side == 1))
        def _():
            send_other(0, 2)

        mirror(sig, 2)
        put_s(0, 1, 1, sig[2])
        cross_new(0)
        newest(0)

        @pl.when(source)
        def _():
            send_other(1, 3)

        @pl.when(side == 1)
        def _():
            own_early(1)

        put_s(1, 1, 1, sig[3])
        cross_new(1)

        @pl.when(source)
        def _():
            send_cross(1)

        newest(1)

        @pl.when(source)
        def _():
            send_newest(0)
            send_newest(1)

    @pl.when(normal & even)
    def _():
        diag_ref[0] = sig[4]
        cross_ref[0] = wf[1, g_half]

    @pl.when(source)
    def _():
        drain(0, LAST)
        drain(1, range(PIECES, KINDS))

    @pl.when(second & source)
    def _():
        drain(0, range(2 * PIECES))
        drain(1, range(PIECES))

    @pl.when(has_next)
    def _():
        drain(2, LAST)

    @pl.when(has_next & jnp.logical_not(right))
    def _():
        drain(2, range(2 * PIECES))

    @pl.when(lower)
    def _():
        drain_packet(0)

    if n >= 32:
        @pl.when(lower)
        def _():
            pl.semaphore_wait(call_sem, 1)

    @pl.when(feeds_sigma)
    def _():
        for copy in sigma_result():
            copy.start()

    @pl.when(feeds_cross)
    def _():
        for copy in cross_result():
            copy.start()
        for copy in cross_result():
            copy.wait_send()

    @pl.when(feeds_sigma)
    def _():
        for copy in sigma_result():
            copy.wait_send()


def body(inv_diag, low_coupling, up_coupling):
    n = lax.axis_size("tm")
    B = inv_diag.shape[1]
    vmem = pl.BlockSpec(memory_space=pltpu.VMEM)
    block = jax.ShapeDtypeStruct(inv_diag.shape, F32)
    return pl.pallas_call(
        functools.partial(kernel, n),
        out_shape=(block, block),
        in_specs=[vmem] * 3,
        out_specs=(vmem, vmem),
        scratch_shapes=[
            pltpu.VMEM((5, B, B), F32),
            pltpu.VMEM((2, 2, B, B), F32),
            pltpu.VMEM((2, 2, B, B), F32),
            pltpu.VMEM((2, 2, B, B), F32),
            pltpu.VMEM((2, B, B), F32),
            pltpu.VMEM((2, B, 2 * B), BF16),
            pltpu.VMEM((2, B, 2 * B), BF16),
            pltpu.VMEM((2, 2 * B, B), BF16),
            pltpu.VMEM((2, 2 * B, B), BF16),
            pltpu.VMEM((2, 2 * B, 2 * B), BF16),
            pltpu.VMEM((2, 2 * B, 2 * B), BF16),
            pltpu.SemaphoreType.DMA((3, 3 * PIECES)),
            pltpu.SemaphoreType.DMA((3 * PIECES,)),
            pltpu.SemaphoreType.DMA((2, PIECES + 6)),
            pltpu.SemaphoreType.DMA((PIECES + 6,)),
            pltpu.SemaphoreType.DMA((PIECES + 3,)),
            pltpu.SemaphoreType.DMA((PIECES + 3,)),
            pltpu.SemaphoreType.REGULAR,
            pltpu.SemaphoreType.REGULAR,
        ],
        compiler_params=pltpu.CompilerParams(
            collective_id=0, has_side_effects=True, vmem_limit_bytes=60 * 1024 * 1024
        ),
    )(inv_diag, low_coupling, up_coupling)


def solution(mesh):
    placed = (P("tm", None, None),) * 3
    return jax.shard_map(
        body,
        mesh=mesh,
        in_specs=placed,
        out_specs=(P("tm", None, None), P("tm", None, None)),
        check_vma=False,
    )
```

```python
import functools

import jax
import jax.numpy as jnp
from jax import lax
from jax.experimental import pallas as pl
from jax.experimental.pallas import tpu as pltpu
from jax.sharding import PartitionSpec as P

MESH = pl.DeviceIdType.MESH
F32 = jnp.float32
BF16 = jnp.bfloat16
row_offset = 3
PIECES = 6


def split(value):
    high = value.astype(BF16)
    return high, (value - high.astype(F32)).astype(BF16)


def mm(a, b):
    return jnp.dot(a, b, preferred_element_type=F32)


def kernel(
    n,
    inv_ref, low_ref, up_ref,
    diag_ref, cross_ref,
    sig, wf, tmp, af, dpk, a_hi, a_lo, at_hi, at_lo, s_hi, s_lo,
    send_sem, recv_sem, pk_send, pk_recv, res_send, res_recv, go_sem, call_sem,
):
    B = inv_ref.shape[1]
    Q = B // 3
    H = B // PIECES
    place = lax.axis_index("tm")
    t = (place + row_offset) % n
    s = jnp.int32(1)
    top_level = n.bit_length() - 2
    even = jnp.bool_(top_level % 2 == 0)
    for k in range(1, n.bit_length() - 1):
        divides = t % (2**k) == 0
        s = jnp.where(divides, 2**k, s)
        even = jnp.where(divides, (top_level - k) % 2 == 0, even)
    is_zero = t == 0
    is_top = t == n // 2
    normal = jnp.logical_not(is_zero)
    odd = jnp.logical_and(normal, jnp.logical_not(even))
    second = jnp.logical_and(jnp.logical_and(normal, even), jnp.logical_not(is_top))
    is_left = jnp.logical_and(t % (4 * s) == s, jnp.logical_not(is_top))
    parent = jnp.where(is_left, t + s, t - s)
    parent_left = parent % (8 * s) == 2 * s
    side = jnp.where(is_left == parent_left, 0, 1)
    half = s // 2
    g_half = jnp.where(is_left, 0, 1)
    to_x = jnp.where(is_left, -1, 1)

    first_round = jnp.logical_and(normal, s >= n // 8)
    source = jnp.logical_and(normal & even, s > 1)
    right = first_round & (t > n // 2)
    lower = jnp.logical_and(second & first_round, is_left)
    late_odd = jnp.logical_and(odd, jnp.logical_not(first_round))
    near = jnp.logical_and(second, side == 1)
    has_next = (near & jnp.logical_not(right)) | (right & (t < 7 * n // 8))
    first_x = t + to_x * jnp.where(is_top, half, half // 2)
    first_p = t - to_x * (half // 2)
    after = jnp.where(right, jnp.where(odd, t - half, t + n // 4), 2 * parent - t)
    before = jnp.where(
        is_top, 0,
        jnp.where(right, jnp.where(odd, n // 2, jnp.where(lower, parent, t - n // 4)), jnp.where(
            near, 2 * t - parent, 2 * parent - t)))
    packet_from = jnp.where(first_round & jnp.logical_not(lower), t - n // 4, parent)
    packet_to = jnp.where(odd & first_round, t - half, jnp.where(lower, t + n // 4, t + to_x * half))
    near_child = t - to_x * half
    feeds_cross = second & is_left
    feeds_sigma = second & (is_left == (s == 1))
    last_odd = odd & (s == 2)
    held = normal & is_left & (s == n // 16) & (t < 3 * n // 4)
    half_held = t == 5 * n // 16
    calls = held & jnp.logical_not(half_held)
    at_start = t == 3 * n // 8
    late_packet = (near & parent_left & (2 * s == n // 16) & (t < 3 * n // 4)) | at_start
    holder = lower | at_start

    bends = n >= 128
    hub = (t % 32 == 10) & bends
    bend_p = near & jnp.logical_not(is_left | first_round) & (s == 4) & bends
    bend_x = second & is_left & jnp.logical_not(near | first_round) & (s == 4) & bends
    bend_q = (s == 16) & normal & bends
    first_x = first_x - jnp.where(bend_q & is_left, 2, 0)
    first_p = first_p - jnp.where(bend_q & jnp.logical_not(is_left), 2, 0)
    before = jnp.where(hub, t + 6, jnp.where(bend_p, t - 2, jnp.where(bend_x, t + 6, before)))
    has_next = has_next & jnp.logical_not(bend_p)
    after = jnp.where(hub, t + 2, after)
    forwards = has_next & jnp.logical_not(late_packet)

    def device(pos):
        return ((pos + (n - row_offset)) % n,)

    ends = (device(first_x), device(first_p), device(after))
    top_dev, start_dev, zero_dev = device(jnp.int32(n // 2)), device(jnp.int32(3 * n // 8)), device(jnp.int32(0))
    held_dev = device(t - n // 16)

    barrier = pltpu.get_barrier_semaphore()

    def greet(dev):
        pl.semaphore_signal(barrier, inc=1, device_id=dev, device_id_type=MESH)

    @pl.when((normal & even) | right | hub)
    def _():
        greet(device(before))

    @pl.when(odd)
    def _():
        greet(device(t - half))

        @pl.when(jnp.logical_not(last_odd))
        def _():
            greet(device(t + half))

    if n >= 32:
        @pl.when(lower)
        def _():
            greet(held_dev)

    @pl.when(second)
    def _():
        greet(device(packet_from))

    @pl.when(at_start)
    def _():
        greet(zero_dev)

    @pl.when(held)
    def _():
        greet(device(parent))

    def number(flag):
        return jnp.where(flag, 1, 0)

    peers = (
        2 * number(is_zero) + 2 * number(source) + number(has_next) + 2 * number(late_odd)
        + number(odd & first_round) + number(lower) + number(feeds_cross) + number(feeds_sigma & (s > 1)) + (number(holder) + number(calls) if n >= 32 else 0) + 2 * number(hub))

    @pl.when(peers > 0)
    def _():
        pl.semaphore_wait(barrier, peers)

    def tri(i):
        start = i * H // Q * Q
        return pl.ds(i * H, H), pl.ds(start, B - start)

    def piece(slot, i, whole):
        return sig.at[slot, pl.ds(i * H, H)] if whole else sig.at[(slot, *tri(i))]

    def copy_to(e, k, src, dst, dev=None):
        return pltpu.make_async_remote_copy(
            src_ref=src, dst_ref=dst, send_sem=send_sem.at[e, k], recv_sem=recv_sem.at[k],
            device_id=ends[e] if dev is None else dev, device_id_type=MESH)

    def target(k):
        return piece(k // PIECES, k % PIECES, k // PIECES == 1)

    def send(e, part, source_of):
        for i in range(PIECES):
            k = part * PIECES + i
            copy_to(e, k, source_of(i), target(k)).start()

    def send_other(e, slot):
        send(e, 0, lambda i: piece(slot, i, False))

    def send_cross(e):
        send(e, 1, lambda i: wf.at[1, e, pl.ds(i * H, H)])

    def send_newest(e):
        send(e, 2, lambda i: piece(4, i, False))

    KINDS = 3 * PIECES

    def packet_parts():
        parts = [(inv_ref.at[(0, *tri(i))], dpk.at[(0, *tri(i))]) for i in range(PIECES)]
        parts += [(af.at[1, i // 3, pl.ds(i % 3 * Q, Q)], af.at[0, i // 3, pl.ds(i % 3 * Q, Q)]) for i in range(6)]
        return parts

    PARTS = PIECES + 6

    def packet(e, k, src, dst, dev):
        return pltpu.make_async_remote_copy(
            src_ref=src, dst_ref=dst, send_sem=pk_send.at[e, k], recv_sem=pk_recv.at[k],
            device_id=dev, device_id_type=MESH)

    def send_packet(e, chosen, dev):
        for k in chosen:
            src, dst = packet_parts()[k]
            packet(e, k, src, dst, dev).start()

    def mirror(ref, slot):
        for i in range(3):
            for j in range(i + 1, 3):
                ref[slot, j * Q:(j + 1) * Q, i * Q:(i + 1) * Q] = ref[slot, i * Q:(i + 1) * Q, j * Q:(j + 1) * Q].T

    def zero_sends():
        out = []
        for i in range(PIECES):
            src = inv_ref.at[(0, *tri(i))]
            out.append(copy_to(0, 2 * PIECES + i, src, target(2 * PIECES + i), top_dev))
        for i in range(PIECES):
            src = inv_ref.at[(0, *tri(i))]
            out.append(copy_to(1, i, src, target(i), start_dev))
        return out

    @pl.when(is_zero)
    def _():
        for copy in zero_sends():
            copy.start()
        diag_ref[...] = inv_ref[...]
        cross_ref[...] = jnp.zeros_like(cross_ref)
        for copy in zero_sends():
            copy.wait_send()

    early = late_odd & jnp.logical_not(held)

    @pl.when(odd)
    def _():
        send_packet(0, range(PIECES), device(packet_to))

    @pl.when(early)
    def _():
        send_packet(1, range(PIECES), device(near_child))

    @pl.when(is_top | right)
    def _():
        sig[0] = jnp.zeros((B, B), F32)
        sig[1] = jnp.zeros((B, B), F32)

    def prepare(i):
        for h in range(2):
            hi, lo = split(af[i, h])
            a_hi[i, :, part(h)] = hi
            a_lo[i, :, part(h)] = lo
            hi_t, lo_t = split(af[i, h].T)
            at_hi[i, part(h), :] = hi_t
            at_lo[i, part(h), :] = lo_t

    def part(h):
        return slice(h * B, (h + 1) * B)

    def put_s(i, row, col, value):
        s_hi[i, part(row), part(col)], s_lo[i, part(row), part(col)] = split(value)

    def three(a, b):
        return mm(a[0], b[0]) + mm(a[0], b[1]) + mm(a[1], b[0])

    def coeff(i, h):
        return a_hi[i, :, part(h)], a_lo[i, :, part(h)]

    def coeff_t(i, h):
        return at_hi[i, part(h), :], at_lo[i, part(h), :]

    def held_s(i, row, col):
        return s_hi[i, part(row), part(col)], s_lo[i, part(row), part(col)]

    def cross_old(i):
        whole = (a_hi[i], a_lo[i])
        wf[i, 0] = -three(whole, (s_hi[i, :, part(0)], s_lo[i, :, part(0)]))

    def partial_new(i):
        tmp[i, 0] = three(coeff(i, 0), held_s(i, 0, 1))

    def partial_sum(i):
        tmp[i, 1] = dpk[i] - three(split(wf[i, 0]), coeff_t(i, 0))

    def cross_new(i):
        wf[i, 1] = -(tmp[i, 0] + three(coeff(i, 1), held_s(i, 1, 1)))

    def newest(i):
        sig[3 + i] = tmp[i, 1] - three(split(wf[i, 1]), coeff_t(i, 1))

    def result(k, src, dst):
        return pltpu.make_async_remote_copy(
            src_ref=src, dst_ref=dst, send_sem=res_send.at[k], recv_sem=res_recv.at[k],
            device_id=device(parent), device_id_type=MESH)

    def sigma_result():
        return [result(i, sig.at[(3, *tri(i))], sig.at[(4, *tri(i))]) for i in range(PIECES)]

    def cross_result():
        own = jnp.where(parent_left, 0, 1)
        return [
            result(PIECES + i, wf.at[0, own, pl.ds(i * Q, Q)], wf.at[1, 0, pl.ds(i * Q, Q)]) for i in range(3)
        ]

    def receive(kinds):
        for k in kinds:
            copy_to(2, k, target(k), target(k)).wait_recv()

            @pl.when(has_next)
            def _():
                copy_to(2, k, target(k), target(k)).start()

    def drain(e, kinds):
        for k in kinds:
            copy_to(e, k, target(k), target(k)).wait_send()

    def drain_packet(e):
        for k, (src, dst) in enumerate(packet_parts()):
            packet(e, k, src, dst, zero_dev).wait_send()

    LAST = range(2 * PIECES, KINDS)

    @pl.when(normal)
    def _():
        dpk[1] = inv_ref[0]
        inverse = split(inv_ref[0])
        for ref, where in ((low_ref, g_half), (up_ref, 1 - g_half)):
            af[1, where] = three(inverse, split(ref[0]))

    @pl.when(odd)
    def _():
        send_packet(0, range(PIECES, PARTS), device(packet_to))

        @pl.when(early)
        def _():
            send_packet(1, range(PIECES, PARTS), device(near_child))

        if n >= 32:
            @pl.when(half_held)
            def _():
                send_packet(1, range(PIECES + 3), device(near_child))

            @pl.when(held)
            def _():
                pl.semaphore_wait(go_sem, 1)

            @pl.when(held & jnp.logical_not(half_held))
            def _():
                send_packet(1, range(PIECES + 3), device(near_child))

            @pl.when(held)
            def _():
                send_packet(1, range(PIECES + 3, PARTS), device(near_child))

        @pl.when(right)
        def _():
            receive(LAST)

        @pl.when(hub)
        def _():
            for k in range(KINDS):
                copy_to(2, k, target(k), target(k)).wait_recv()
                copy_to(2, k, target(k), target(k)).start()
                copy_to(0, k, target(k), target(k), device(t - 6)).start()
            drain(2, range(KINDS))
            drain(0, range(KINDS))

        for copy in sigma_result() + cross_result():
            copy.wait_recv()

        if n >= 32:
            @pl.when(calls)
            def _():
                pl.semaphore_signal(call_sem, inc=1, device_id=device(parent), device_id_type=MESH)

        mirror(sig, 4)
        diag_ref[0] = sig[4]
        cross_ref[0] = wf[1, 0]
        drain_packet(0)

        @pl.when(late_odd)
        def _():
            drain_packet(1)

    @pl.when(is_top)
    def _():
        prepare(1)
        receive(LAST)
        mirror(sig, 2)
        put_s(1, 1, 1, sig[2])
        wf[1, 0] = jnp.zeros((B, B), F32)
        tmp[1, 0] = jnp.zeros((B, B), F32)
        tmp[1, 1] = inv_ref[0]
        cross_new(1)
        send_cross(1)
        newest(1)
        send_newest(0)
        send_newest(1)

    @pl.when(second)
    def _():
        prepare(1)

        def get_packet():
            for k, (_, dst) in enumerate(packet_parts()):
                packet(0, k, dst, dst, zero_dev).wait_recv()

                @pl.when(lower)
                def _():
                    packet(0, k, dst, dst, device(packet_to)).start()

            mirror(dpk, 0)
            prepare(0)

        def go():
            pl.semaphore_signal(go_sem, inc=1, device_id=held_dev, device_id_type=MESH)

        @pl.when(jnp.logical_not(late_packet))
        def _():
            get_packet()

        if n >= 32:
            @pl.when(lower)
            def _():
                go()

        @pl.when(jnp.logical_not(right))
        def _():
            receive(range(2 * PIECES))

        @pl.when(late_packet)
        def _():
            receive(LAST)

            if n >= 32:
                @pl.when(at_start)
                def _():
                    go()

            get_packet()

        def pass_on(kinds):
            @pl.when(forwards)
            def _():
                receive(kinds)

        @pl.when(source & (side == 0))
        def _():
            send_other(0, 0)

        mirror(sig, 0)
        put_s(0, 0, 0, sig[0])
        put_s(0, 1, 0, sig[1])
        put_s(0, 0, 1, sig[1].T)
        pass_on(LAST[:1])
        cross_old(0)
        pass_on(LAST[1:2])
        partial_new(0)
        pass_on(LAST[2:3])
        partial_sum(0)

        def own_early(block):
            span = pl.ds(pl.multiple_of(block * B, B), B)
            s_hi[1, part(0), part(0)] = s_hi[0, span, span]
            s_lo[1, part(0), part(0)] = s_lo[0, span, span]
            put_s(1, 1, 0, wf[0, block])
            put_s(1, 0, 1, wf[0, block].T)
            partial_new(1)

        ahead = (side == 0) & (s == 1)

        @pl.when(ahead)
        def _():
            own_early(0)
            cross_old(1)
            partial_sum(1)

        pass_on(LAST[3:])

        @pl.when(jnp.logical_not(forwards | late_packet))
        def _():
            receive(LAST)

        @pl.when(source & (side == 1))
        def _():
            send_other(0, 2)

        mirror(sig, 2)
        put_s(0, 1, 1, sig[2])
        cross_new(0)
        newest(0)

        @pl.when(source)
        def _():
            send_other(1, 3)

        @pl.when(jnp.logical_not(ahead))
        def _():
            own_early(side)

        put_s(1, 1, 1, sig[3])
        cross_new(1)

        @pl.when(source)
        def _():
            send_cross(1)

        @pl.when(jnp.logical_not(ahead))
        def _():
            cross_old(1)

            @pl.when(source)
            def _():
                send_cross(0)

            partial_sum(1)

        newest(1)

        @pl.when(source)
        def _():
            send_newest(0)
            send_newest(1)

    @pl.when(normal & even)
    def _():
        diag_ref[0] = sig[4]
        cross_ref[0] = wf[1, g_half]

    @pl.when(source)
    def _():
        drain(0, LAST)
        drain(1, range(PIECES, KINDS))

    @pl.when(second & source)
    def _():
        drain(0, range(2 * PIECES))
        drain(1, range(PIECES))

    @pl.when(has_next)
    def _():
        drain(2, LAST)

    @pl.when(has_next & jnp.logical_not(right))
    def _():
        drain(2, range(2 * PIECES))

    @pl.when(lower)
    def _():
        drain_packet(0)

    if n >= 32:
        @pl.when(lower)
        def _():
            pl.semaphore_wait(call_sem, 1)

    @pl.when(feeds_sigma)
    def _():
        for copy in sigma_result():
            copy.start()

    @pl.when(feeds_cross)
    def _():
        for copy in cross_result():
            copy.start()
        for copy in cross_result():
            copy.wait_send()

    @pl.when(feeds_sigma)
    def _():
        for copy in sigma_result():
            copy.wait_send()


def body(inv_diag, low_coupling, up_coupling):
    n = lax.axis_size("tm")
    B = inv_diag.shape[1]
    vmem = pl.BlockSpec(memory_space=pltpu.VMEM)
    block = jax.ShapeDtypeStruct(inv_diag.shape, F32)
    return pl.pallas_call(
        functools.partial(kernel, n),
        out_shape=(block, block),
        in_specs=[vmem] * 3,
        out_specs=(vmem, vmem),
        scratch_shapes=[
            pltpu.VMEM((5, B, B), F32),
            pltpu.VMEM((2, 2, B, B), F32),
            pltpu.VMEM((2, 2, B, B), F32),
            pltpu.VMEM((2, 2, B, B), F32),
            pltpu.VMEM((2, B, B), F32),
            pltpu.VMEM((2, B, 2 * B), BF16),
            pltpu.VMEM((2, B, 2 * B), BF16),
            pltpu.VMEM((2, 2 * B, B), BF16),
            pltpu.VMEM((2, 2 * B, B), BF16),
            pltpu.VMEM((2, 2 * B, 2 * B), BF16),
            pltpu.VMEM((2, 2 * B, 2 * B), BF16),
            pltpu.SemaphoreType.DMA((3, 3 * PIECES)),
            pltpu.SemaphoreType.DMA((3 * PIECES,)),
            pltpu.SemaphoreType.DMA((2, PIECES + 6)),
            pltpu.SemaphoreType.DMA((PIECES + 6,)),
            pltpu.SemaphoreType.DMA((PIECES + 3,)),
            pltpu.SemaphoreType.DMA((PIECES + 3,)),
            pltpu.SemaphoreType.REGULAR,
            pltpu.SemaphoreType.REGULAR,
        ],
        compiler_params=pltpu.CompilerParams(
            collective_id=0, has_side_effects=True, vmem_limit_bytes=60 * 1024 * 1024
        ),
    )(inv_diag, low_coupling, up_coupling)


def solution(mesh):
    placed = (P("tm", None, None),) * 3
    return jax.shard_map(
        body,
        mesh=mesh,
        in_specs=placed,
        out_specs=(P("tm", None, None), P("tm", None, None)),
        check_vma=False,
    )
```

```python
import functools

import jax
import jax.numpy as jnp
from jax import lax
from jax.experimental import pallas as pl
from jax.experimental.pallas import tpu as pltpu
from jax.sharding import PartitionSpec as P

MESH = pl.DeviceIdType.MESH
F32 = jnp.float32
BF16 = jnp.bfloat16
row_offset = 3
PIECES = 6


def split(value):
    high = value.astype(BF16)
    return high, (value - high.astype(F32)).astype(BF16)


def mm(a, b):
    return jnp.dot(a, b, preferred_element_type=F32)


def kernel(
    n,
    inv_hbm, low_hbm, up_hbm,
    diag_ref, cross_ref,
    inv_ref, low_ref, up_ref, load_sem, sig, wf, tmp, af, dpk, a_hi, a_lo, at_hi, at_lo, s_hi, s_lo,
    send_sem, recv_sem, pk_send, pk_recv, res_send, res_recv, go_sem, call_sem,
):
    B = inv_ref.shape[1]
    loads = [
        pltpu.make_async_copy(src, dst, load_sem.at[k])
        for k, (src, dst) in enumerate(((inv_hbm, inv_ref), (low_hbm, low_ref), (up_hbm, up_ref)))
    ]
    for load in loads:
        load.start()
    Q = B // 3
    H = B // PIECES
    place = lax.axis_index("tm")
    t = (place + row_offset) % n
    s = jnp.int32(1)
    top_level = n.bit_length() - 2
    even = jnp.bool_(top_level % 2 == 0)
    for k in range(1, n.bit_length() - 1):
        divides = t % (2**k) == 0
        s = jnp.where(divides, 2**k, s)
        even = jnp.where(divides, (top_level - k) % 2 == 0, even)
    is_zero = t == 0
    is_top = t == n // 2
    normal = jnp.logical_not(is_zero)
    odd = jnp.logical_and(normal, jnp.logical_not(even))
    second = jnp.logical_and(jnp.logical_and(normal, even), jnp.logical_not(is_top))
    is_left = jnp.logical_and(t % (4 * s) == s, jnp.logical_not(is_top))
    parent = jnp.where(is_left, t + s, t - s)
    parent_left = parent % (8 * s) == 2 * s
    side = jnp.where(is_left == parent_left, 0, 1)
    half = s // 2
    g_half = jnp.where(is_left, 0, 1)
    to_x = jnp.where(is_left, -1, 1)

    first_round = jnp.logical_and(normal, s >= n // 8)
    source = jnp.logical_and(normal & even, s > 1)
    right = first_round & (t > n // 2)
    lower = jnp.logical_and(second & first_round, is_left)
    late_odd = jnp.logical_and(odd, jnp.logical_not(first_round))
    near = jnp.logical_and(second, side == 1)
    has_next = (near & jnp.logical_not(right)) | (right & (t < 7 * n // 8))
    first_x = t + to_x * jnp.where(is_top, half, half // 2)
    first_p = t - to_x * (half // 2)
    after = jnp.where(right, jnp.where(odd, t - half, t + n // 4), 2 * parent - t)
    before = jnp.where(
        is_top, 0,
        jnp.where(right, jnp.where(odd, n // 2, jnp.where(lower, parent, t - n // 4)), jnp.where(
            near, 2 * t - parent, 2 * parent - t)))
    packet_from = jnp.where(first_round & jnp.logical_not(lower), t - n // 4, parent)
    packet_to = jnp.where(odd & first_round, t - half, jnp.where(lower, t + n // 4, t + to_x * half))
    near_child = t - to_x * half
    feeds_cross = second & is_left
    feeds_sigma = second & (is_left == (s == 1))
    last_odd = odd & (s == 2)
    held = normal & is_left & (s == n // 16) & (t < 3 * n // 4)
    half_held = t == 5 * n // 16
    calls = held & jnp.logical_not(half_held)
    at_start = t == 3 * n // 8
    late_packet = (near & parent_left & (2 * s == n // 16) & (t < 3 * n // 4) & (parent != 5 * n // 16)) | at_start
    holder = lower | at_start

    bends = n >= 128
    hub = (t % 32 == 10) & bends
    bend_p = near & jnp.logical_not(is_left | first_round) & (s == 4) & bends
    bend_x = second & is_left & jnp.logical_not(near | first_round) & (s == 4) & bends
    bend_q = (s == 16) & normal & bends
    first_x = first_x - jnp.where(bend_q & is_left, 2, 0)
    first_p = first_p - jnp.where(bend_q & jnp.logical_not(is_left), 2, 0)
    before = jnp.where(hub, t + 6, jnp.where(bend_p, t - 2, jnp.where(bend_x, t + 6, before)))
    has_next = has_next & jnp.logical_not(bend_p)
    after = jnp.where(hub, t + 2, after)
    forwards = has_next & jnp.logical_not(late_packet)

    def device(pos):
        return ((pos + (n - row_offset)) % n,)

    ends = (device(first_x), device(first_p), device(after))
    top_dev, start_dev, zero_dev = device(jnp.int32(n // 2)), device(jnp.int32(3 * n // 8)), device(jnp.int32(0))
    held_dev = device(t - n // 16)

    barrier = pltpu.get_barrier_semaphore()

    def greet(dev):
        pl.semaphore_signal(barrier, inc=1, device_id=dev, device_id_type=MESH)

    @pl.when((normal & even) | right | hub)
    def _():
        greet(device(before))

    @pl.when(odd)
    def _():
        greet(device(t - half))

        @pl.when(jnp.logical_not(last_odd))
        def _():
            greet(device(t + half))

    if n >= 32:
        @pl.when(lower)
        def _():
            greet(held_dev)

    @pl.when(second)
    def _():
        greet(device(packet_from))

    @pl.when(at_start)
    def _():
        greet(zero_dev)

    @pl.when(held)
    def _():
        greet(device(parent))

    def number(flag):
        return jnp.where(flag, 1, 0)

    peers = (
        2 * number(is_zero) + 2 * number(source) + number(has_next) + 2 * number(late_odd)
        + number(odd & first_round) + number(lower) + number(feeds_cross) + number(feeds_sigma & (s > 1)) + (number(holder) + number(calls) if n >= 32 else 0) + 2 * number(hub))

    @pl.when(peers > 0)
    def _():
        pl.semaphore_wait(barrier, peers)

    for load in loads:
        load.wait()

    def tri(i):
        start = i * H // Q * Q
        return pl.ds(i * H, H), pl.ds(start, B - start)

    def piece(slot, i, whole):
        return sig.at[slot, pl.ds(i * H, H)] if whole else sig.at[(slot, *tri(i))]

    def copy_to(e, k, src, dst, dev=None):
        return pltpu.make_async_remote_copy(
            src_ref=src, dst_ref=dst, send_sem=send_sem.at[e, k], recv_sem=recv_sem.at[k],
            device_id=ends[e] if dev is None else dev, device_id_type=MESH)

    def target(k):
        return piece(k // PIECES, k % PIECES, k // PIECES == 1)

    def send(e, part, source_of):
        for i in range(PIECES):
            k = part * PIECES + i
            copy_to(e, k, source_of(i), target(k)).start()

    def send_other(e, slot):
        send(e, 0, lambda i: piece(slot, i, False))

    def send_cross(e):
        send(e, 1, lambda i: wf.at[1, e, pl.ds(i * H, H)])

    def send_newest(e):
        send(e, 2, lambda i: piece(4, i, False))

    KINDS = 3 * PIECES

    def packet_parts():
        parts = [(inv_ref.at[(0, *tri(i))], dpk.at[(0, *tri(i))]) for i in range(PIECES)]
        parts += [(af.at[1, i // 3, pl.ds(i % 3 * Q, Q)], af.at[0, i // 3, pl.ds(i % 3 * Q, Q)]) for i in range(6)]
        return parts

    PARTS = PIECES + 6

    def packet(e, k, src, dst, dev):
        return pltpu.make_async_remote_copy(
            src_ref=src, dst_ref=dst, send_sem=pk_send.at[e, k], recv_sem=pk_recv.at[k],
            device_id=dev, device_id_type=MESH)

    def send_packet(e, chosen, dev):
        for k in chosen:
            src, dst = packet_parts()[k]
            packet(e, k, src, dst, dev).start()

    def mirror(ref, slot):
        for i in range(3):
            for j in range(i + 1, 3):
                ref[slot, j * Q:(j + 1) * Q, i * Q:(i + 1) * Q] = ref[slot, i * Q:(i + 1) * Q, j * Q:(j + 1) * Q].T

    def zero_sends():
        out = []
        for i in range(PIECES):
            src = inv_ref.at[(0, *tri(i))]
            out.append(copy_to(0, 2 * PIECES + i, src, target(2 * PIECES + i), top_dev))
        for i in range(PIECES):
            src = inv_ref.at[(0, *tri(i))]
            out.append(copy_to(1, i, src, target(i), start_dev))
        return out

    @pl.when(is_zero)
    def _():
        for copy in zero_sends():
            copy.start()
        diag_ref[...] = inv_ref[...]
        cross_ref[...] = jnp.zeros_like(cross_ref)
        for copy in zero_sends():
            copy.wait_send()

    early = late_odd & jnp.logical_not(held)

    @pl.when(odd)
    def _():
        send_packet(0, range(PIECES), device(packet_to))

    @pl.when(early)
    def _():
        send_packet(1, range(PIECES), device(near_child))

    @pl.when(is_top | right)
    def _():
        sig[0] = jnp.zeros((B, B), F32)
        sig[1] = jnp.zeros((B, B), F32)

    def prepare(i):
        for h in range(2):
            hi, lo = split(af[i, h])
            a_hi[i, :, part(h)] = hi
            a_lo[i, :, part(h)] = lo
            hi_t, lo_t = split(af[i, h].T)
            at_hi[i, part(h), :] = hi_t
            at_lo[i, part(h), :] = lo_t

    def part(h):
        return slice(h * B, (h + 1) * B)

    def put_s(i, row, col, value):
        s_hi[i, part(row), part(col)], s_lo[i, part(row), part(col)] = split(value)

    def three(a, b):
        return mm(a[0], b[0]) + mm(a[0], b[1]) + mm(a[1], b[0])

    def coeff(i, h):
        return a_hi[i, :, part(h)], a_lo[i, :, part(h)]

    def coeff_t(i, h):
        return at_hi[i, part(h), :], at_lo[i, part(h), :]

    def held_s(i, row, col):
        return s_hi[i, part(row), part(col)], s_lo[i, part(row), part(col)]

    def cross_old(i):
        whole = (a_hi[i], a_lo[i])
        wf[i, 0] = -three(whole, (s_hi[i, :, part(0)], s_lo[i, :, part(0)]))

    def partial_new(i):
        tmp[i, 0] = three(coeff(i, 0), held_s(i, 0, 1))

    def partial_sum(i):
        tmp[i, 1] = dpk[i] - three(split(wf[i, 0]), coeff_t(i, 0))

    def cross_new(i):
        wf[i, 1] = -(tmp[i, 0] + three(coeff(i, 1), held_s(i, 1, 1)))

    def newest(i):
        sig[3 + i] = tmp[i, 1] - three(split(wf[i, 1]), coeff_t(i, 1))

    def result(k, src, dst):
        return pltpu.make_async_remote_copy(
            src_ref=src, dst_ref=dst, send_sem=res_send.at[k], recv_sem=res_recv.at[k],
            device_id=device(parent), device_id_type=MESH)

    def sigma_result():
        return [result(i, sig.at[(3, *tri(i))], sig.at[(4, *tri(i))]) for i in range(PIECES)]

    def cross_result():
        own = jnp.where(parent_left, 0, 1)
        return [
            result(PIECES + i, wf.at[0, own, pl.ds(i * Q, Q)], wf.at[1, 0, pl.ds(i * Q, Q)]) for i in range(3)
        ]

    def receive(kinds):
        for k in kinds:
            copy_to(2, k, target(k), target(k)).wait_recv()

            @pl.when(has_next)
            def _():
                copy_to(2, k, target(k), target(k)).start()

    def drain(e, kinds):
        for k in kinds:
            copy_to(e, k, target(k), target(k)).wait_send()

    def drain_packet(e):
        for k, (src, dst) in enumerate(packet_parts()):
            packet(e, k, src, dst, zero_dev).wait_send()

    LAST = range(2 * PIECES, KINDS)

    @pl.when(normal)
    def _():
        dpk[1] = inv_ref[0]
        inverse = split(inv_ref[0])
        for ref, where in ((low_ref, g_half), (up_ref, 1 - g_half)):
            af[1, where] = three(inverse, split(ref[0]))

    @pl.when(odd)
    def _():
        send_packet(0, range(PIECES, PARTS), device(packet_to))

        @pl.when(early)
        def _():
            send_packet(1, range(PIECES, PARTS), device(near_child))

        if n >= 32:
            @pl.when(half_held)
            def _():
                send_packet(1, range(PIECES + 3), device(near_child))

            @pl.when(held)
            def _():
                pl.semaphore_wait(go_sem, 1)

            @pl.when(held & jnp.logical_not(half_held))
            def _():
                send_packet(1, range(PIECES + 3), device(near_child))

            @pl.when(held)
            def _():
                send_packet(1, range(PIECES + 3, PARTS), device(near_child))

        @pl.when(right)
        def _():
            receive(LAST)

        @pl.when(hub)
        def _():
            for k in range(KINDS):
                copy_to(2, k, target(k), target(k)).wait_recv()
                copy_to(2, k, target(k), target(k)).start()
                copy_to(0, k, target(k), target(k), device(t - 6)).start()
            drain(2, range(KINDS))
            drain(0, range(KINDS))

        for copy in sigma_result() + cross_result():
            copy.wait_recv()

        if n >= 32:
            @pl.when(calls)
            def _():
                pl.semaphore_signal(call_sem, inc=1, device_id=device(parent), device_id_type=MESH)

        mirror(sig, 4)
        diag_ref[0] = sig[4]
        cross_ref[0] = wf[1, 0]
        drain_packet(0)

        @pl.when(late_odd)
        def _():
            drain_packet(1)

    @pl.when(is_top)
    def _():
        prepare(1)
        receive(LAST)
        mirror(sig, 2)
        put_s(1, 1, 1, sig[2])
        wf[1, 0] = jnp.zeros((B, B), F32)
        tmp[1, 0] = jnp.zeros((B, B), F32)
        tmp[1, 1] = inv_ref[0]
        cross_new(1)
        send_cross(1)
        newest(1)
        send_newest(0)
        send_newest(1)

    @pl.when(second)
    def _():
        prepare(1)

        def get_packet():
            for k, (_, dst) in enumerate(packet_parts()):
                packet(0, k, dst, dst, zero_dev).wait_recv()

                @pl.when(lower)
                def _():
                    packet(0, k, dst, dst, device(packet_to)).start()

            mirror(dpk, 0)
            prepare(0)

        def go():
            pl.semaphore_signal(go_sem, inc=1, device_id=held_dev, device_id_type=MESH)

        @pl.when(jnp.logical_not(late_packet))
        def _():
            get_packet()

        if n >= 32:
            @pl.when(lower)
            def _():
                go()

        @pl.when(jnp.logical_not(right))
        def _():
            receive(range(2 * PIECES))

        @pl.when(late_packet)
        def _():
            receive(LAST)

            if n >= 32:
                @pl.when(at_start)
                def _():
                    go()

            get_packet()

        def pass_on(kinds):
            @pl.when(forwards)
            def _():
                receive(kinds)

        @pl.when(source & (side == 0))
        def _():
            send_other(0, 0)

        mirror(sig, 0)
        put_s(0, 0, 0, sig[0])
        put_s(0, 1, 0, sig[1])
        put_s(0, 0, 1, sig[1].T)
        pass_on(LAST[:1])
        cross_old(0)
        pass_on(LAST[1:2])
        partial_new(0)
        pass_on(LAST[2:3])
        partial_sum(0)

        def own_early(block):
            span = pl.ds(pl.multiple_of(block * B, B), B)
            s_hi[1, part(0), part(0)] = s_hi[0, span, span]
            s_lo[1, part(0), part(0)] = s_lo[0, span, span]
            put_s(1, 1, 0, wf[0, block])
            put_s(1, 0, 1, wf[0, block].T)
            partial_new(1)

        ahead = (side == 0) & (s == 1)

        @pl.when(ahead)
        def _():
            own_early(0)
            cross_old(1)
            partial_sum(1)

        pass_on(LAST[3:])

        @pl.when(jnp.logical_not(forwards | late_packet))
        def _():
            receive(LAST)

        @pl.when(source & (side == 1))
        def _():
            send_other(0, 2)

        mirror(sig, 2)
        put_s(0, 1, 1, sig[2])
        cross_new(0)
        newest(0)

        @pl.when(source)
        def _():
            send_other(1, 3)

        @pl.when(jnp.logical_not(ahead))
        def _():
            own_early(side)

        put_s(1, 1, 1, sig[3])
        cross_new(1)

        @pl.when(source)
        def _():
            send_cross(1)

        @pl.when(jnp.logical_not(ahead))
        def _():
            cross_old(1)

            @pl.when(source)
            def _():
                send_cross(0)

            partial_sum(1)

        newest(1)

        @pl.when(source)
        def _():
            send_newest(0)
            send_newest(1)

    @pl.when(normal & even)
    def _():
        diag_ref[0] = sig[4]
        cross_ref[0] = wf[1, g_half]

    @pl.when(source)
    def _():
        drain(0, LAST)
        drain(1, range(PIECES, KINDS))

    @pl.when(second & source)
    def _():
        drain(0, range(2 * PIECES))
        drain(1, range(PIECES))

    @pl.when(has_next)
    def _():
        drain(2, LAST)

    @pl.when(has_next & jnp.logical_not(right))
    def _():
        drain(2, range(2 * PIECES))

    @pl.when(lower)
    def _():
        drain_packet(0)

    if n >= 32:
        @pl.when(lower)
        def _():
            pl.semaphore_wait(call_sem, 1)

    @pl.when(feeds_sigma)
    def _():
        for copy in sigma_result():
            copy.start()

    @pl.when(feeds_cross)
    def _():
        for copy in cross_result():
            copy.start()
        for copy in cross_result():
            copy.wait_send()

    @pl.when(feeds_sigma)
    def _():
        for copy in sigma_result():
            copy.wait_send()


def body(inv_diag, low_coupling, up_coupling):
    n = lax.axis_size("tm")
    B = inv_diag.shape[1]
    vmem = pl.BlockSpec(memory_space=pltpu.VMEM)
    block = jax.ShapeDtypeStruct(inv_diag.shape, F32)
    return pl.pallas_call(
        functools.partial(kernel, n),
        out_shape=(block, block),
        in_specs=[pl.BlockSpec(memory_space=pl.ANY)] * 3,
        out_specs=(vmem, vmem),
        scratch_shapes=[
            pltpu.VMEM((1, B, B), F32),
            pltpu.VMEM((1, B, B), F32),
            pltpu.VMEM((1, B, B), F32),
            pltpu.SemaphoreType.DMA((3,)),
            pltpu.VMEM((5, B, B), F32),
            pltpu.VMEM((2, 2, B, B), F32),
            pltpu.VMEM((2, 2, B, B), F32),
            pltpu.VMEM((2, 2, B, B), F32),
            pltpu.VMEM((2, B, B), F32),
            pltpu.VMEM((2, B, 2 * B), BF16),
            pltpu.VMEM((2, B, 2 * B), BF16),
            pltpu.VMEM((2, 2 * B, B), BF16),
            pltpu.VMEM((2, 2 * B, B), BF16),
            pltpu.VMEM((2, 2 * B, 2 * B), BF16),
            pltpu.VMEM((2, 2 * B, 2 * B), BF16),
            pltpu.SemaphoreType.DMA((3, 3 * PIECES)),
            pltpu.SemaphoreType.DMA((3 * PIECES,)),
            pltpu.SemaphoreType.DMA((2, PIECES + 6)),
            pltpu.SemaphoreType.DMA((PIECES + 6,)),
            pltpu.SemaphoreType.DMA((PIECES + 3,)),
            pltpu.SemaphoreType.DMA((PIECES + 3,)),
            pltpu.SemaphoreType.REGULAR,
            pltpu.SemaphoreType.REGULAR,
        ],
        compiler_params=pltpu.CompilerParams(
            collective_id=0, has_side_effects=True, vmem_limit_bytes=54_900_000
        ),
    )(inv_diag, low_coupling, up_coupling)


def solution(mesh):
    placed = (P("tm", None, None),) * 3
    return jax.shard_map(
        body,
        mesh=mesh,
        in_specs=placed,
        out_specs=(P("tm", None, None), P("tm", None, None)),
        check_vma=False,
    )
```
